128 devices in a mesh: gx: 8 (over y, core), gy: 8 (over x, z_hi), gz: 2 (over z_lo).
Axes of the slice: x: 4, y: 4, z: 4 (z_hi: 2, z_lo: 2; z = z_hi * 2 + z_lo), core: 2. Of those that a mesh axis runs over, the one named last changes fastest.
Arguments:
- positions: float32 [8, 8, 2, 3, 512], P('gx', 'gy', 'gz'), may hold values from 0 to 1
- attributes: bfloat16 [8, 8, 2, 512, 128], P('gx', 'gy', 'gz'), may hold values from -6 to 6
- edge_center: int32 [8, 8, 2, 6144], P('gx', 'gy', 'gz'), may hold values from 0 to 511
- edge_other: int32 [8, 8, 2, 6144], P('gx', 'gy', 'gz'), may hold values from 0 to 2687
- edge_count: int32 [8, 8, 2], P('gx', 'gy', 'gz'), may hold values from 1536 to 6144, as said below
- rim_rows: int32 [8, 8, 2, 8, 128], P('gx', 'gy', 'gz'), may hold values from 0 to 511
- z_rows: int32 [8, 8, 2, 128], P('gx', 'gy', 'gz'), may hold values from 0 to 2559
- w_emb: bfloat16 [128, 256], replicated, may hold values from -0.5 to 0.5
- w_rbf: float32 [8, 256], replicated, may hold values from -2 to 2
- w_chan: bfloat16 [256, 64], replicated, may hold values from -0.375 to 0.375
- w_lat: bfloat16 [256, 256], replicated, may hold values from -0.375 to 0.375
- w_ten: bfloat16 [192, 256], replicated, may hold values from -0.4375 to 0.4375
- w_out: float32 [256], replicated, may hold values from -0.375 to 0.375
Outputs:
- atom_energy: float32 [8, 8, 2, 512], P('gx', 'gy', 'gz')
- forces: float32 [8, 8, 2, 3, 512], P('gx', 'gy', 'gz')
The draws below stay inside these ranges and needn't reach their ends.
Inputs may be any that keep to these rules, and one draw needn't show every extreme that they name: `edge_count`: a multiple of 128; a device's edge slots below its count are live; some device has 6144.
All inputs are finite; a program needn't handle non-finite values.
Results may differ from the reference program's by a relative error of at most 0.005.
Values may be sent and summed in bfloat16 or wider, within the bound.
A program may use at most 64 MiB of HBM per device.

```python
import jax
import jax.numpy as jnp
from jax import lax

F = 256
CH = 64
ADIM = 128
NB = 8
ATOMS = 512
EDGES = 6144
RIM = 128
ZROWS = 128
TBL = 2688
N_GX = 8
N_GY = 8
N_GZ = 2


def draw_edge_count(key, part):
    blocks_all = EDGES // 128
    lowest = EDGES // 512
    devices = N_GX * N_GY * N_GZ
    key_first, key_second, key_third = jax.random.split(key, 3)
    draw_first = jax.random.randint(key_first, (devices,), lowest, blocks_all + 1)
    draw_second = jax.random.randint(key_second, (devices,), lowest, blocks_all + 1)
    picked = jnp.minimum(draw_first, draw_second)
    busiest = jax.random.randint(key_third, (), 0, devices)
    picked = jnp.where(jnp.arange(devices) == busiest, blocks_all, picked)
    return (picked * 128).reshape(N_GX, N_GY, N_GZ).astype(jnp.int32)


def with_ends(values, rng, smallest, largest):
    extent = values.shape
    index_at = [jax.random.randint(jax.random.fold_in(rng, axis), (), 0, extent[axis]) for axis in range(len(extent))]
    values = values.at[tuple(index_at)].set(smallest)
    longest = extent.index(max(extent))
    index_at[longest] = (index_at[longest] + 1) % extent[longest]
    return values.at[tuple(index_at)].set(largest)


def levels(own_key, extent, shards, least, high):
    loudness = 1.0
    for axis_at, blocks in shards:
        steps = jax.random.uniform(jax.random.fold_in(jax.random.fold_in(own_key, 6), axis_at), (blocks,), jnp.float32, least / len(shards), high / len(shards))
        loudness = loudness * jnp.repeat(jnp.exp(steps), extent[axis_at] // blocks).reshape((-1,) + (1,) * (len(extent) - 1 - axis_at))
    return loudness


def bell_draw(key, shape, deviation, reach, shards=(), dtype=jnp.bfloat16):
    entries = jax.random.normal(key, shape, jnp.float32) * deviation
    if len(shards) > 0:
        entries = levels(key, shape, shards, -0.22, 0.18) * entries
    return jnp.clip(entries, min=-reach, max=reach).astype(dtype)


def setup_inputs(seed: int = 0) -> dict:
    streams_of = jax.random.split(jax.random.key(seed), 14)
    positions = jnp.clip(1.0 * jax.random.uniform(streams_of[0], (N_GX, N_GY, N_GZ, 3, ATOMS), jnp.float32) ** levels(streams_of[0], (N_GX, N_GY, N_GZ, 3, ATOMS), ((0, 8), (1, 8), (2, 2)), -0.2, 0.2), 0.0, 1.0)
    attributes = bell_draw(streams_of[1], (N_GX, N_GY, N_GZ, ATOMS, ADIM), 1.0, 6.0, ((0, 8), (1, 8), (2, 2)))
    edge_center = with_ends(jax.random.randint(streams_of[2], (N_GX, N_GY, N_GZ, EDGES), 0, ATOMS), jax.random.fold_in(streams_of[2], 1), 0, ATOMS - 1).astype(jnp.int32)
    edge_other = with_ends(jax.random.randint(streams_of[3], (N_GX, N_GY, N_GZ, EDGES), 0, TBL), jax.random.fold_in(streams_of[3], 1), 0, TBL - 1).astype(jnp.int32)
    edge_count = draw_edge_count(jax.random.fold_in(streams_of[13], 71), 0)
    rim_rows = with_ends(jax.random.randint(streams_of[5], (N_GX, N_GY, N_GZ, 8, RIM), 0, ATOMS), jax.random.fold_in(streams_of[5], 1), 0, ATOMS - 1).astype(jnp.int32)
    z_rows = with_ends(jax.random.randint(streams_of[6], (N_GX, N_GY, N_GZ, ZROWS), 0, ATOMS + 16 * RIM), jax.random.fold_in(streams_of[6], 1), 0, (ATOMS + 16 * RIM) - 1).astype(jnp.int32)
    w_emb = bell_draw(streams_of[7], (ADIM, F), ADIM ** -0.5, 0.5)
    w_rbf = bell_draw(streams_of[8], (NB, F), NB ** -0.5, 2.0, (), jnp.float32)
    w_chan = bell_draw(streams_of[9], (F, CH), F ** -0.5, 0.375)
    w_lat = bell_draw(streams_of[10], (F, F), F ** -0.5, 0.375)
    w_ten = bell_draw(streams_of[11], (3 * CH, F), (3 * CH) ** -0.5, 0.4375)
    w_out = bell_draw(streams_of[12], (F,), F ** -0.5, 0.375, (), jnp.float32)
    return dict(positions=positions, attributes=attributes, edge_center=edge_center, edge_other=edge_other, edge_count=edge_count, rim_rows=rim_rows, z_rows=z_rows, w_emb=w_emb, w_rbf=w_rbf, w_chan=w_chan, w_lat=w_lat, w_ten=w_ten, w_out=w_out)


rim_cells = [(0, 0), (0, 1), (0, 2), (1, 0), (1, 2), (2, 0), (2, 1), (2, 2)]
cycle_cells = [(cycle_row, cycle_column) for cycle_row in range(5) for cycle_column in range(5) if cycle_row in (0, 4) or cycle_column in (0, 4)]

def source_of(position):
    if position == 0:
        return (-1, 2)
    if position == 4:
        return (1, 0)
    return (0, position - 1)

def embed_atoms(atom_rows, w_emb):
    return jax.nn.silu(jnp.dot(atom_rows, w_emb, preferred_element_type=jnp.float32)).astype(jnp.bfloat16)

def split_join(values):
    upper = lax.optimization_barrier(values.astype(jnp.bfloat16))
    lower = (values - upper.astype(jnp.float32)).astype(jnp.bfloat16)
    return upper.astype(jnp.float32) + lower.astype(jnp.float32)

def harmonics(directions):
    along_x, along_y, along_z = (directions[0], directions[1], directions[2])
    root_three = 3.0 ** 0.5
    return [jnp.ones_like(along_x), along_x, along_y, along_z, root_three * along_x * along_y, root_three * along_y * along_z, root_three * along_z * along_x, 0.5 * root_three * (along_x * along_x - along_y * along_y), 0.5 * (3.0 * along_z * along_z - 1.0)]

def latent_of(position_table, feature_table, centers, others, w_rbf):
    separation = position_table[:, others] - position_table[:, centers]
    squared = lax.optimization_barrier(jnp.sum(separation * separation, axis=0))
    distance = jnp.sqrt(squared + 0.25)
    directions = separation / distance[None, :]
    envelope = 1.0 / (1.0 + squared * squared / 16.0)
    radii = 0.5 + 0.4 * jnp.arange(w_rbf.shape[0]).astype(jnp.float32)
    radial = jnp.exp(-jnp.square((distance[None, :] - radii[:, None]) / 0.5)) * envelope[None, :]
    mixed = lax.dot_general(radial, w_rbf, (((0,), (0,)), ((), ())), precision=lax.Precision.HIGHEST, preferred_element_type=jnp.float32)
    mixed = mixed + feature_table[centers].astype(jnp.float32) + feature_table[others].astype(jnp.float32)
    return (jax.nn.silu(mixed).astype(jnp.bfloat16), directions, envelope)

def tensor_terms(latent, directions, centers, live_mask, w_chan, atom_count):
    channel = jnp.dot(latent, w_chan, preferred_element_type=jnp.float32) * live_mask[:, None]
    harmonic = harmonics(directions)
    products = jnp.concatenate([channel * term[:, None] for term in harmonic], axis=1)
    return jax.ops.segment_sum(products, centers, num_segments=atom_count)

def energy_terms(latent, directions, envelope, tensor, centers, live_mask, w_lat, w_ten, w_out):
    harmonic = harmonics(directions)
    gathered = tensor[centers]
    width = gathered.shape[1] // 9
    bands = []
    for lower, upper in ((0, 1), (1, 4), (4, 9)):
        band = gathered[:, lower * width:(lower + 1) * width] * harmonic[lower][:, None]
        for index in range(lower + 1, upper):
            band = band + gathered[:, index * width:(index + 1) * width] * harmonic[index][:, None]
        bands.append(band)
    invariant = jnp.concatenate(bands, axis=1).astype(jnp.bfloat16)
    hidden = jax.nn.silu(jnp.dot(latent, w_lat, preferred_element_type=jnp.float32) + jnp.dot(invariant, w_ten, preferred_element_type=jnp.float32))
    return lax.optimization_barrier(jnp.sum(hidden * w_out[None, :], axis=1)) * envelope * live_mask

def reference(positions, attributes, edge_center, edge_other, edge_count, rim_rows, z_rows, w_emb, w_rbf, w_chan, w_lat, w_ten, w_out):
    grid_shape = (N_GX, N_GY, N_GZ)
    devices = N_GX * N_GY * N_GZ
    embedded = embed_atoms(attributes.reshape(-1, ADIM), w_emb).reshape(grid_shape + (ATOMS, F))
    rim_flat = rim_rows.reshape(devices, 8 * RIM)
    rim_features = jax.vmap(lambda atom_table, row_index: atom_table[row_index])(embedded.reshape(devices, ATOMS, F), rim_flat).reshape(grid_shape + (8, RIM, F))
    rim_positions = split_join(jax.vmap(lambda atom_table, row_index: atom_table[:, row_index])(positions.reshape(devices, 3, ATOMS), rim_flat)).reshape(grid_shape + (3, 8, RIM))
    cycle_features = []
    cycle_positions = []
    for cycle_row, cycle_column in cycle_cells:
        shift_x, cell_row = source_of(cycle_row)
        shift_y, cell_column = source_of(cycle_column)
        rim_index = rim_cells.index((cell_row, cell_column))
        cycle_features.append(jnp.roll(rim_features[:, :, :, rim_index], (-shift_x, -shift_y), axis=(0, 1)))
        shifted = jnp.roll(rim_positions[:, :, :, :, rim_index], (-shift_x, -shift_y), axis=(0, 1))
        cycle_positions.append(shifted + jnp.array([shift_x, shift_y, 0], jnp.float32)[:, None])
    inner_features = jnp.concatenate([embedded] + cycle_features, axis=3)
    inner_positions = jnp.concatenate([positions] + cycle_positions, axis=4)
    inner_len = ATOMS + 16 * RIM
    slab_flat = z_rows.reshape(devices, ZROWS)
    slab_features = jax.vmap(lambda atom_table, row_index: atom_table[row_index])(inner_features.reshape(devices, inner_len, F), slab_flat).reshape(grid_shape + (ZROWS, F))
    slab_positions = split_join(jax.vmap(lambda atom_table, row_index: atom_table[:, row_index])(inner_positions.reshape(devices, 3, inner_len), slab_flat)).reshape(grid_shape + (3, ZROWS))
    slab_features = jnp.roll(slab_features, 1, axis=2)
    slab_positions = jnp.roll(slab_positions, 1, axis=2)
    slab_lift = (1 - 2 * jnp.arange(N_GZ)).astype(jnp.float32)
    slab_positions = slab_positions.at[:, :, :, 2].add(slab_lift[None, None, :, None])
    feature_table = jnp.concatenate([inner_features, slab_features], axis=3).reshape(devices, TBL, F)
    position_table = jnp.concatenate([inner_positions, slab_positions], axis=4).reshape(devices, 3, TBL)

    def device_pass(items):
        place_table, embed_table, centers, others, live_count = items
        live_mask = (jnp.arange(centers.shape[0]) < live_count).astype(jnp.float32)

        def total_energy(place_values):
            latent, directions, envelope = latent_of(place_values, embed_table, centers, others, w_rbf)
            tensor = 0.125 * tensor_terms(latent, directions, centers, live_mask, w_chan, ATOMS)
            edge_energy = energy_terms(latent, directions, envelope, tensor, centers, live_mask, w_lat, w_ten, w_out)
            return (jnp.sum(edge_energy), jax.ops.segment_sum(edge_energy, centers, num_segments=ATOMS))
        total, pullback, atom_values = jax.vjp(total_energy, place_table, has_aux=True)
        gradient = pullback(jnp.ones_like(total))[0]
        return (atom_values, gradient)
    atom_energy, gradient = lax.map(device_pass, (position_table, feature_table, edge_center.reshape(devices, EDGES), edge_other.reshape(devices, EDGES), edge_count.reshape(devices)))
    gradient = gradient.reshape(grid_shape + (3, TBL))
    slab_grad = jnp.roll(gradient[..., inner_len:], 1, axis=2).reshape(devices, 3, ZROWS)
    inner_grad = jax.vmap(lambda grads, row_index, values: grads.at[:, row_index].add(values))(gradient[..., :inner_len].reshape(devices, 3, inner_len), slab_flat, slab_grad).reshape(grid_shape + (3, inner_len))
    own_grad = inner_grad[..., :ATOMS]
    cycle_grad = inner_grad[..., ATOMS:].reshape(grid_shape + (3, 16, RIM))
    rim_grad = jnp.zeros(grid_shape + (3, 8, RIM), jnp.float32)
    for cycle_index, (cycle_row, cycle_column) in enumerate(cycle_cells):
        shift_x, cell_row = source_of(cycle_row)
        shift_y, cell_column = source_of(cycle_column)
        rim_index = rim_cells.index((cell_row, cell_column))
        rim_grad = rim_grad.at[:, :, :, :, rim_index].add(jnp.roll(cycle_grad[:, :, :, :, cycle_index], (shift_x, shift_y), axis=(0, 1)))
    own_grad = jax.vmap(lambda grads, row_index, values: grads.at[:, row_index].add(values))(own_grad.reshape(devices, 3, ATOMS), rim_flat, rim_grad.reshape(devices, 3, 8 * RIM))
    return (atom_energy.reshape(grid_shape + (ATOMS,)), (-own_grad).reshape(grid_shape + (3, ATOMS)))
```

```python
import functools

import jax
import jax.numpy as jnp
from jax import lax
from jax.experimental import pallas as pl
from jax.experimental.pallas import tpu as pltpu
from jax.sharding import PartitionSpec as P

F32, BF16, I32 = jnp.float32, jnp.bfloat16, jnp.int32
ROOT3 = 3.0 ** 0.5
BANDS = (0, 1, 1, 1, 2, 2, 2, 2, 2)


def nt(a, b):
    return lax.dot_general(a, b, (((1,), (1,)), ((), ())), preferred_element_type=F32)


def nn(a, b):
    return jnp.dot(a, b, preferred_element_type=F32)


def turned(w, unit):
    return lax.dot_general(w, unit, (((0,), (0,)), ((), ())), preferred_element_type=F32).astype(BF16)


def sigmoid(x):
    return 0.5 * jnp.tanh(0.5 * x) + 0.5


def eye(n):
    rows = lax.broadcasted_iota(I32, (n, n), 0)
    cols = lax.broadcasted_iota(I32, (n, n), 1)
    return jnp.where(rows == cols, 1.0, 0.0).astype(BF16)


def three_parts(v):
    upper = v.astype(BF16).astype(F32)
    rest = v - upper
    middle = rest.astype(BF16).astype(F32)
    return upper, middle, rest - middle


def hits(rows, index_row, offset, width):
    ids = lax.broadcasted_iota(I32, (rows, width), 0) + offset
    return jnp.where(ids == index_row, 1.0, 0.0).astype(BF16)


def edge_kernel(
    attr_ref, pos_ref, center_ref, other_ref, w_emb_ref, w_rbf_ref, w_chan_ref, w_lat_ref, w_ten_ref,
    w_out_ref, energy_ref, grad_ref,
    tab, one_c, lat_s, dsilu_s, dlat_s, chan_s, geo_s, dh_s, tens, tens_b, wrt, wct, wlt, wtt, wback, wr2, wout_c,
    *, nb, eb, atoms, tbl,
):
    feat = w_emb_ref.shape[1]
    adim = w_emb_ref.shape[0]
    ch = w_chan_ref.shape[1]
    nbas = w_rbf_ref.shape[0]
    big_eye = eye(feat)
    emb_t = turned(w_emb_ref[...], eye(adim))
    wct[...] = turned(w_chan_ref[...], big_eye)
    wlt[...] = turned(w_lat_ref[...], big_eye)
    wtt[...] = turned(w_ten_ref[...], eye(3 * ch))
    wback[0:feat, :] = w_lat_ref[...]
    wback[feat:, :] = w_ten_ref[...]
    rb = w_rbf_ref[...]
    rb_hi = rb.astype(BF16).astype(F32)
    rb_lo = rb - rb_hi
    wr2[...] = jnp.concatenate([rb_hi, rb_lo], axis=0).astype(BF16)
    wrt[...] = nt(big_eye, jnp.concatenate([rb_hi, rb_hi, rb_lo, rb_lo], axis=0).astype(BF16)).astype(BF16)
    wo = w_out_ref[...]
    wout_c[...] = jnp.sum(jnp.where(
        lax.broadcasted_iota(I32, (feat, feat), 0) == lax.broadcasted_iota(I32, (feat, feat), 1),
        jnp.broadcast_to(wo, (feat, feat)), 0.0), axis=1, keepdims=True)

    emb = nn(emb_t, attr_ref[...])
    emb = (emb * sigmoid(emb)).astype(BF16)
    tab[0:feat, 0:tbl] = emb
    tab[0:feat, tbl:] = emb[:, 0:atoms]
    p3 = three_parts(pos_ref[...][0:3])
    rows = jnp.concatenate(list(p3) + [jnp.zeros((7, tbl), F32)], axis=0)
    tab[feat:, 0:tbl] = rows.astype(BF16)
    tab[feat:, tbl:] = (-rows[:, 0:atoms]).astype(BF16)

    tens[...] = jnp.zeros_like(tens)

    def geometry(sep):
        sq = jnp.sum(sep * sep, axis=0, keepdims=True)
        inv = lax.rsqrt(sq + 0.25)
        dist = (sq + 0.25) * inv
        env = 1.0 / (1.0 + sq * sq * (1.0 / 16.0))
        radii = 0.5 + 0.4 * lax.broadcasted_iota(I32, (nbas, 1), 0).astype(F32)
        t = (dist - radii) * 2.0
        gauss = jnp.exp(-(t * t))
        return sq, inv, dist, env, t, gauss

    def phase1(b, _):
        c_row = center_ref[b]
        o_row = other_ref[b]
        a_o = hits(tbl, o_row, 0, eb)
        a_c = hits(atoms, c_row, 0, eb)
        one_c[b] = a_c
        m1 = nn(tab[:, 0:tbl], a_o) + nn(tab[:, tbl:], a_c)
        sep = m1[feat:feat + 3] + m1[feat + 3:feat + 6] + m1[feat + 6:feat + 9]
        sq, inv, dist, env, t, gauss = geometry(sep)
        radial = gauss * env
        r_hi = radial.astype(BF16).astype(F32)
        r_lo = radial - r_hi
        parts = jnp.concatenate([r_hi, r_lo, r_hi, r_lo], axis=0).astype(BF16)
        mixed = m1[0:feat] + nn(wrt[...], parts)
        s = sigmoid(mixed)
        latent = (mixed * s).astype(BF16)
        lat_s[b] = latent
        dsilu_s[b] = (s * (1.0 + mixed * (1.0 - s))).astype(BF16)
        chan = nn(wct[...], latent)
        chan_s[b] = chan
        dirs = sep * inv
        x, y, z = dirs[0:1], dirs[1:2], dirs[2:3]
        harm = jnp.concatenate([
            jnp.ones_like(x), x, y, z, ROOT3 * x * y, ROOT3 * y * z, ROOT3 * z * x,
            0.5 * ROOT3 * (x * x - y * y), 0.5 * (3.0 * z * z - 1.0),
            sep, env, jnp.zeros((3, eb), F32)], axis=0)
        geo_s[b] = harm
        prod = jnp.concatenate([chan] + [chan * harm[m:m + 1] for m in range(1, 9)], axis=0).astype(BF16)
        tens[0:9 * ch] += nt(prod, a_c)
        return 0

    lax.fori_loop(0, nb, phase1, 0)
    tens_b[...] = (0.125 * tens[0:9 * ch]).astype(BF16)
    tens[...] = jnp.zeros_like(tens)

    def phase2(b, _):
        a_c = one_c[b]
        harm = geo_s[b]
        env = harm[12:13]
        latent = lat_s[b]
        gath = nn(tens_b[...], a_c)
        g = [gath[m * ch:(m + 1) * ch] for m in range(9)]
        h = [harm[m:m + 1] for m in range(9)]
        inv0 = g[0]
        inv1 = g[1] * h[1] + g[2] * h[2] + g[3] * h[3]
        inv2 = g[4] * h[4] + g[5] * h[5] + g[6] * h[6] + g[7] * h[7] + g[8] * h[8]
        invb = jnp.concatenate([inv0, inv1, inv2], axis=0).astype(BF16)
        pre = nn(wlt[...], latent) + nn(wtt[...], invb)
        s = sigmoid(pre)
        wo = wout_c[...]
        e = jnp.sum(pre * s * wo, axis=0, keepdims=True)
        dpre = (s * (1.0 + pre * (1.0 - s))) * wo * env
        back = nn(wback[...], dpre.astype(BF16))
        dlat_s[b] = back[0:feat]
        dinv = [back[feat + l * ch:feat + (l + 1) * ch] for l in range(3)]
        dh = [jnp.sum(dinv[BANDS[m]] * g[m], axis=0, keepdims=True) for m in range(1, 9)]
        en = e * env
        dh_s[b] = jnp.concatenate([e] + dh + [jnp.zeros((7, eb), F32)], axis=0)
        en_hi = en.astype(BF16).astype(F32)
        prod = jnp.concatenate(
            [dinv[0]] + [dinv[BANDS[m]] * h[m] for m in range(1, 9)] + [en_hi, en - en_hi, jnp.zeros((14, eb), F32)],
            axis=0).astype(BF16)
        tens[...] += nt(prod, a_c)
        return 0

    lax.fori_loop(0, nb, phase2, 0)
    energy_ref[...] = tens[9 * ch:9 * ch + 1] + tens[9 * ch + 1:9 * ch + 2]
    tens_b[...] = (0.125 * tens[0:9 * ch]).astype(BF16)
    grad_ref[...] = jnp.zeros_like(grad_ref)
    nqo, nqc = tbl // 128, atoms // 128

    def phase3(b, _):
        a_c = one_c[b]
        harm = geo_s[b]
        gd = nn(tens_b[...], a_c)
        g = [gd[m * ch:(m + 1) * ch] for m in range(9)]
        h = [harm[m:m + 1] for m in range(9)]
        chan = chan_s[b]
        dchan = g[0]
        for m in range(1, 9):
            dchan = dchan + g[m] * h[m]
        old = dh_s[b]
        k = [None] + [old[m:m + 1] + jnp.sum(chan * g[m], axis=0, keepdims=True) for m in range(1, 9)]
        dlat = dlat_s[b] + nn(w_chan_ref[...], dchan.astype(BF16))
        dmixed = (dlat * dsilu_s[b].astype(F32)).astype(BF16)
        d16 = nn(wr2[...], dmixed)
        drad = d16[0:nbas] + d16[nbas:]
        sep = harm[9:12]
        sq, inv, dist, env, t, gauss = geometry(sep)
        dg = drad * gauss
        d_dist = jnp.sum(dg * t, axis=0, keepdims=True) * (-4.0 * env)
        d_env = jnp.sum(dg, axis=0, keepdims=True) + old[0:1]
        x, y, z = h[1], h[2], h[3]
        dx = k[1] + ROOT3 * (y * k[4] + z * k[6] + x * k[7])
        dy = k[2] + ROOT3 * (x * k[4] + z * k[5] - y * k[7])
        dz = k[3] + ROOT3 * (y * k[5] + x * k[6]) + 3.0 * z * k[8]
        d_dist = d_dist - (dx * x + dy * y + dz * z) * inv
        d_sq = d_dist * (0.5 * inv) - d_env * env * env * sq * 0.125
        dsep = jnp.concatenate([dx, dy, dz], axis=0) * inv + sep * (2.0 * d_sq)
        hi = dsep.astype(BF16).astype(F32)
        d8 = jnp.concatenate([hi, dsep - hi, jnp.zeros((2, eb), F32)], axis=0)
        o_row, c_row = other_ref[b], center_ref[b]
        oq, cq = o_row >> 7, c_row >> 7
        lhs = jnp.concatenate(
            [jnp.where(oq == q, d8, 0.0) for q in range(nqo)] + [jnp.where(cq == q, d8, 0.0) for q in range(nqc)],
            axis=0).astype(BF16)
        rhs = jnp.concatenate([hits(128, o_row & 127, 0, eb), hits(128, c_row & 127, 0, eb)], axis=0)
        grad_ref[...] += nt(lhs, rhs)
        return 0

    lax.fori_loop(0, nb, phase3, 0)


def edge_call(attr_t, pos8, centers, others, w_emb, w_rbf, w_chan, w_lat, w_ten, w_out, eb=512):
    feat, ch, tbl, atoms = w_emb.shape[1], w_chan.shape[1], attr_t.shape[1], 512
    edges = centers.shape[0]
    nb = edges // eb
    V = pltpu.VMEM
    spec = pl.BlockSpec(memory_space=pltpu.VMEM)
    return pl.pallas_call(
        functools.partial(edge_kernel, nb=nb, eb=eb, atoms=atoms, tbl=tbl),
        out_shape=(jax.ShapeDtypeStruct((1, atoms), F32), jax.ShapeDtypeStruct(((tbl + atoms) // 128 * 8, 256), F32)),
        in_specs=[spec] * 10, out_specs=(spec, spec),
        scratch_shapes=[
            V((feat + 16, tbl + atoms), BF16), V((nb, atoms, eb), BF16), V((nb, feat, eb), BF16), V((nb, feat, eb), BF16),
            V((nb, feat, eb), F32), V((nb, ch, eb), F32), V((nb, 16, eb), F32), V((nb, 16, eb), F32),
            V((9 * ch + 16, atoms), F32), V((9 * ch, atoms), BF16),
            V((feat, 32), BF16), V((ch, feat), BF16), V((feat, feat), BF16), V((feat, 3 * ch), BF16),
            V((feat + 3 * ch, feat), BF16), V((16, feat), BF16), V((feat, 1), F32)],
        compiler_params=pltpu.CompilerParams(vmem_limit_bytes=60 << 20),
        name="edges",
    )(attr_t, pos8, centers.reshape(nb, 1, eb), others.reshape(nb, 1, eb), w_emb, w_rbf, w_chan, w_lat, w_ten, w_out.reshape(1, -1))


MESH = pl.DeviceIdType.MESH
RIM_CELLS = [(0, 0), (0, 1), (0, 2), (1, 0), (1, 2), (2, 0), (2, 1), (2, 2)]


def source_of(position):
    if position == 0:
        return (-1, 2)
    if position == 4:
        return (1, 0)
    return (0, position - 1)


LINKS = []
for row in range(5):
    for column in range(5):
        if row in (0, 4) or column in (0, 4):
            sx, ra = source_of(row)
            sy, rb = source_of(column)
            LINKS.append((len(LINKS), RIM_CELLS.index((ra, rb)), sx, sy))
SEND_ORDER = sorted(LINKS, key=lambda link: -(3 * abs(link[3]) + abs(link[2])))


def places():
    i, j, k = (lax.axis_index(name) for name in ("gx", "gy", "gz"))
    nx, ny = lax.axis_size("gx"), lax.axis_size("gy")

    def at(sx, sy):
        return (lax.rem(i + (sx + nx), nx), lax.rem(j + (sy + ny), ny), k)

    return at, (i, j, 1 - k), k


def greet(at, partner):
    barrier = pltpu.get_barrier_semaphore()
    for sx in (-1, 0, 1):
        for sy in (-1, 0, 1):
            if sx or sy:
                pl.semaphore_signal(barrier, inc=1, device_id=at(sx, sy), device_id_type=MESH)
    pl.semaphore_signal(barrier, inc=1, device_id=partner, device_id_type=MESH)
    pl.semaphore_wait(barrier, 9)


def two_parts(v):
    upper = v.astype(BF16).astype(F32)
    return upper, v - upper


def table_kernel(
    attr_ref, pos_ref, rim_ref, z_ref, table_ref, place_ref,
    cells, got, zcell, zgot, inner, send_sem, recv_sem, zsend, zrecv,
):
    at, partner, k = places()
    adim, atoms = attr_ref.shape[1], attr_ref.shape[0]
    rim_len = rim_ref.shape[1]
    attr_t = nt(eye(adim), attr_ref[...])
    pos = pos_ref[...]
    hi, lo = two_parts(pos)
    pad = jnp.zeros((10, atoms), F32)
    own = jnp.concatenate([attr_t, hi, lo, pad], axis=0).astype(BF16)
    inner[:, 0:atoms] = own
    table_ref[:, 0:atoms] = own[0:adim]
    place_ref[:, 0:atoms] = jnp.concatenate([pos, jnp.zeros((5, atoms), F32)], axis=0)
    for c in range(8):
        cells[c] = nn(own, hits(atoms, rim_ref[c:c + 1, :], 0, rim_len)).astype(BF16)
    greet(at, partner)

    def link_copy(slot, cell, sx, sy):
        return pltpu.make_async_remote_copy(
            src_ref=cells.at[cell], dst_ref=got.at[slot], send_sem=send_sem.at[slot], recv_sem=recv_sem.at[slot],
            device_id=at(-sx, -sy), device_id_type=MESH)

    for link in SEND_ORDER:
        link_copy(*link).start()
    for slot, cell, sx, sy in SEND_ORDER[::-1]:
        link_copy(slot, cell, sx, sy).wait_recv()
        block = got[slot]
        first = atoms + slot * rim_len
        table_ref[:, first:first + rim_len] = block[0:adim]
        tail = block[adim:].astype(F32)
        rows = lax.broadcasted_iota(I32, (3, rim_len), 0)
        shift = jnp.where(rows == 0, float(sx), jnp.where(rows == 1, float(sy), 0.0))
        moved = tail[0:3] + tail[3:6] + shift
        place_ref[:, first:first + rim_len] = jnp.concatenate([moved, jnp.zeros((5, rim_len), F32)], axis=0)
        hi, lo = two_parts(moved)
        inner[0:adim, first:first + rim_len] = block[0:adim]
        inner[adim:, first:first + rim_len] = jnp.concatenate([hi, lo, pad[:, 0:rim_len]], axis=0).astype(BF16)
    inner_len = inner.shape[1]
    zlen = z_ref.shape[1]
    zcell[...] = nn(inner[...], hits(inner_len, z_ref[...], 0, zlen)).astype(BF16)
    zcopy = pltpu.make_async_remote_copy(
        src_ref=zcell, dst_ref=zgot, send_sem=zsend, recv_sem=zrecv, device_id=partner, device_id_type=MESH)
    zcopy.start()
    zcopy.wait_recv()
    block = zgot[...]
    table_ref[:, inner_len:] = block[0:adim]
    tail = block[adim:].astype(F32)
    lift = (1 - 2 * k).astype(F32)
    rows = lax.broadcasted_iota(I32, (3, zlen), 0)
    moved = tail[0:3] + tail[3:6] + jnp.where(rows == 2, lift, 0.0)
    place_ref[:, inner_len:] = jnp.concatenate([moved, jnp.zeros((5, zlen), F32)], axis=0)
    for link in LINKS:
        link_copy(*link).wait_send()
    zcopy.wait_send()


def table_call(attr, pos, rim, z):
    atoms, adim = attr.shape
    rim_len, zlen = rim.shape[1], z.shape[1]
    inner_len = atoms + 16 * rim_len
    V, D = pltpu.VMEM, pltpu.SemaphoreType.DMA
    spec = pl.BlockSpec(memory_space=pltpu.VMEM)
    return pl.pallas_call(
        table_kernel,
        out_shape=(jax.ShapeDtypeStruct((adim, inner_len + zlen), BF16), jax.ShapeDtypeStruct((8, inner_len + zlen), F32)),
        in_specs=[spec] * 4, out_specs=(spec, spec),
        scratch_shapes=[
            V((8, adim + 16, rim_len), BF16), V((16, adim + 16, rim_len), BF16), V((adim + 16, zlen), BF16),
            V((adim + 16, zlen), BF16), V((adim + 16, inner_len), BF16), D((16,)), D((16,)), D, D],
        compiler_params=pltpu.CompilerParams(collective_id=0, has_side_effects=True, vmem_limit_bytes=32 << 20),
        name="table",
    )(attr, pos, rim, z)


def force_kernel(
    grad_ref, rim_ref, z_ref, force_ref,
    slab, slab_got, cells, got, send_sem, recv_sem, zsend, zrecv,
):
    at, partner, k = places()
    atoms = force_ref.shape[1]
    rim_len, zlen = rim_ref.shape[1], z_ref.shape[1]
    nqc = atoms // 128
    nqo = grad_ref.shape[0] // 8 - nqc

    def summed(block):
        return block[0:3] + block[3:6]

    slab[...] = grad_ref[(nqo - 1) * 8:nqo * 8, 0:128]
    greet(at, partner)
    zcopy = pltpu.make_async_remote_copy(
        src_ref=slab, dst_ref=slab_got, send_sem=zsend, recv_sem=zrecv, device_id=partner, device_id_type=MESH)
    zcopy.start()
    own = jnp.concatenate(
        [summed(grad_ref[q * 8:(q + 1) * 8, 0:128]) - summed(grad_ref[(nqo + q) * 8:(nqo + q + 1) * 8, 128:256])
         for q in range(nqc)], axis=1)
    zcopy.wait_recv()
    back = jnp.concatenate(list(three_parts(summed(slab_got[...]))) + [jnp.zeros((7, zlen), F32)], axis=0).astype(BF16)
    z_row = z_ref[...]
    own_back = nt(back, hits(atoms, z_row, 0, zlen))
    own = own + own_back[0:3] + own_back[3:6] + own_back[6:9]
    spread = nt(back, hits(16 * rim_len, z_row, atoms, zlen))
    spread = spread[0:3] + spread[3:6] + spread[6:9]
    for slot in range(16):
        q = nqc + slot
        cells[slot, 0:3] = summed(grad_ref[q * 8:(q + 1) * 8, 0:128]) + spread[:, slot * rim_len:(slot + 1) * rim_len]
        cells[slot, 3:8] = jnp.zeros((5, rim_len), F32)

    def link_copy(slot, cell, sx, sy):
        return pltpu.make_async_remote_copy(
            src_ref=cells.at[slot], dst_ref=got.at[slot], send_sem=send_sem.at[slot], recv_sem=recv_sem.at[slot],
            device_id=at(sx, sy), device_id_type=MESH)

    for link in SEND_ORDER:
        link_copy(*link).start()
    for link in SEND_ORDER[::-1]:
        link_copy(*link).wait_recv()
    rim_back = []
    for cell in range(8):
        rim_back.append(sum(got[slot][0:3] for slot, c, sx, sy in LINKS if c == cell))
    total = jnp.concatenate(rim_back, axis=1)
    parts = jnp.concatenate(list(three_parts(total)) + [jnp.zeros((7, 8 * rim_len), F32)], axis=0).astype(BF16)
    for cell in range(8):
        add = nt(parts[:, cell * rim_len:(cell + 1) * rim_len], hits(atoms, rim_ref[cell:cell + 1, :], 0, rim_len))
        own = own + add[0:3] + add[3:6] + add[6:9]
    force_ref[...] = -own
    for link in LINKS:
        link_copy(*link).wait_send()
    zcopy.wait_send()


def force_call(grad, rim, z, atoms):
    rim_len, zlen = rim.shape[1], z.shape[1]
    V, D = pltpu.VMEM, pltpu.SemaphoreType.DMA
    spec = pl.BlockSpec(memory_space=pltpu.VMEM)
    return pl.pallas_call(
        force_kernel,
        out_shape=jax.ShapeDtypeStruct((3, atoms), F32),
        in_specs=[spec] * 3, out_specs=spec,
        scratch_shapes=[
            V((8, zlen), F32), V((8, zlen), F32), V((16, 8, rim_len), F32), V((16, 8, rim_len), F32),
            D((16,)), D((16,)), D, D],
        compiler_params=pltpu.CompilerParams(collective_id=1, has_side_effects=True, vmem_limit_bytes=32 << 20),
        name="forces",
    )(grad, rim, z)


def per_device(
    positions, attributes, edge_center, edge_other, edge_count, rim_rows, z_rows, w_emb, w_rbf, w_chan, w_lat, w_ten, w_out,
):
    rim = rim_rows[0, 0, 0]
    z = z_rows[0, 0]
    live = jnp.arange(edge_center.shape[3]) < edge_count[0, 0, 0]
    centers = jnp.where(live, edge_center[0, 0, 0], -1)
    others = jnp.where(live, edge_other[0, 0, 0], -1)
    attr_t, pos8 = table_call(attributes[0, 0, 0], positions[0, 0, 0], rim, z)
    energy, grad = edge_call(attr_t, pos8, centers, others, w_emb, w_rbf, w_chan, w_lat, w_ten, w_out)
    forces = force_call(grad, rim, z, positions.shape[4])
    return energy.reshape(1, 1, 1, -1), forces[None, None, None]


def solution(mesh):
    spread = P("gx", "gy", "gz")
    return jax.shard_map(
        per_device,
        mesh=mesh,
        in_specs=(spread,) * 7 + (P(),) * 6,
        out_specs=(spread, spread),
        check_vma=False,
    )
```

```python
import functools

import jax
import jax.numpy as jnp
from jax import lax
from jax.experimental import pallas as pl
from jax.experimental.pallas import tpu as pltpu
from jax.sharding import PartitionSpec as P

F32, BF16, I32 = jnp.float32, jnp.bfloat16, jnp.int32
ROOT3 = 3.0 ** 0.5
BANDS = (0, 1, 1, 1, 2, 2, 2, 2, 2)
BLOCK = 2048
VMEM_LIMIT = 62 << 20
MESH = pl.DeviceIdType.MESH
RIM_CELLS = [(0, 0), (0, 1), (0, 2), (1, 0), (1, 2), (2, 0), (2, 1), (2, 2)]


def source_of(position):
    if position == 0:
        return (-1, 2)
    if position == 4:
        return (1, 0)
    return (0, position - 1)


NEAR = [(0, 1), (0, -1), (1, 1), (1, -1), (-1, 1), (-1, -1), (1, 0), (-1, 0)]
CELLS = {shift: [] for shift in NEAR}
slots = 0
for row in range(5):
    for column in range(5):
        if row in (0, 4) or column in (0, 4):
            sx, ra = source_of(row)
            sy, rb = source_of(column)
            CELLS[sx, sy].append((slots, RIM_CELLS.index((ra, rb))))
            slots += 1
SLOT_ORDER = [slot for shift in NEAR for slot, _ in CELLS[shift]]


def nt(a, b):
    return lax.dot_general(a, b, (((1,), (1,)), ((), ())), preferred_element_type=F32)


def nn(a, b):
    return jnp.dot(a, b, preferred_element_type=F32)


def turned(w, unit):
    return lax.dot_general(w, unit, (((0,), (0,)), ((), ())), preferred_element_type=F32).astype(BF16)


def sigmoid(x):
    return 0.5 * jnp.tanh(0.5 * x) + 0.5


def eye(n):
    rows = lax.broadcasted_iota(I32, (n, n), 0)
    cols = lax.broadcasted_iota(I32, (n, n), 1)
    return jnp.where(rows == cols, 1.0, 0.0).astype(BF16)


def three_parts(v):
    upper = v.astype(BF16).astype(F32)
    rest = v - upper
    middle = rest.astype(BF16).astype(F32)
    return upper, middle, rest - middle


def hits(rows, index_row, offset):
    width = index_row.shape[1]
    ids = lax.broadcasted_iota(jnp.int16, (rows, width), 0)
    wanted = jnp.broadcast_to((index_row - offset).astype(jnp.int16), (rows, width))
    return jnp.where(ids == wanted, jnp.ones((), BF16), jnp.zeros((), BF16))


def whole_kernel(
    pos_ref, attr_ref, center_ref, other_ref, count_ref, rim_ref, z_ref,
    w_emb_ref, w_rbf_ref, w_chan_ref, w_lat_ref, w_ten_ref, w_out_ref,
    energy_ref, force_ref,
    tab, acc, one_c, lat_s, dsilu_s, chan_s, geo_s, dh_s, index_s, tens, tens_b, grad,
    emb_t, wrt, wchan, wcat, wback, wr2, wout_c, rim_hits,
    cells, got, inner, zcell, zgot, zlist, zback, zback_got, back_got,
    send_sem, recv_sem, zsend, zrecv, bsend, brecv, zbsend, zbrecv,
    *, block,
):
    adim, feat = w_emb_ref.shape
    ch, nbas = w_chan_ref.shape[0], w_rbf_ref.shape[0]
    atoms, edges = attr_ref.shape[0], center_ref.shape[1]
    rim_len, zlen = rim_ref.shape[1], z_ref.shape[1]
    inner_len = atoms + 16 * rim_len
    tbl = inner_len + zlen
    nb = edges // block
    nqc = atoms // 128

    i, j, k = (lax.axis_index(name) for name in ("gx", "gy", "gz"))
    nx, ny = lax.axis_size("gx"), lax.axis_size("gy")

    def at(sx, sy, side):
        return (lax.rem(i + (sx + nx), nx), lax.rem(j + (sy + ny), ny), side)

    partner = (i, j, 1 - k)
    barrier = pltpu.get_barrier_semaphore()
    for sx, sy in NEAR:
        pl.semaphore_signal(barrier, inc=1, device_id=at(sx, sy, k), device_id_type=MESH)
        pl.semaphore_signal(barrier, inc=1, device_id=at(sx, sy, 1 - k), device_id_type=MESH)
    pl.semaphore_signal(barrier, inc=1, device_id=partner, device_id_type=MESH)

    pos = jnp.concatenate([pos_ref[0], pos_ref[1], pos_ref[2]], axis=0)
    upper = pos.astype(BF16).astype(F32)
    own = jnp.concatenate(
        [nt(eye(adim), attr_ref[...]), upper, pos - upper, jnp.zeros((10, atoms), F32)], axis=0).astype(BF16)
    inner[:, 0:atoms] = own
    rim_row = jnp.concatenate([rim_ref[c:c + 1, :] for c in range(8)], axis=1)
    rim_hits[...] = hits(atoms, rim_row, 0)
    packed = nn(own, rim_hits[...]).astype(BF16)
    for n, shift in enumerate(NEAR):
        for m, (_, cell) in enumerate(CELLS[shift]):
            cells[n, m] = packed[:, cell * rim_len:(cell + 1) * rim_len]
    pl.semaphore_wait(barrier, 17)

    def rim_copy(n):
        sx, sy = NEAR[n]
        count = len(CELLS[sx, sy])
        return pltpu.make_async_remote_copy(
            src_ref=cells.at[n, 0:count], dst_ref=got.at[n, 0:count], send_sem=send_sem.at[n], recv_sem=recv_sem.at[n],
            device_id=at(-sx, -sy, k), device_id_type=MESH)

    for n in range(8):
        rim_copy(n).start()

    big_eye = eye(feat)
    emb_t[...] = turned(w_emb_ref[...], eye(adim))
    wchan[...] = turned(w_chan_ref[...], eye(ch))
    wcat[:, 0:feat] = turned(w_lat_ref[...], big_eye)
    wcat[:, feat:] = turned(w_ten_ref[...], eye(3 * ch))
    wback[0:feat, :] = w_lat_ref[...]
    wback[feat:, :] = w_ten_ref[...]
    rb = w_rbf_ref[...]
    rb_hi = rb.astype(BF16).astype(F32)
    rb_lo = rb - rb_hi
    wr2[...] = jnp.concatenate([rb_hi, rb_lo], axis=0).astype(BF16)
    wrt[...] = nt(big_eye, jnp.concatenate([rb_hi, rb_hi, rb_lo, rb_lo], axis=0).astype(BF16)).astype(BF16)
    diagonal = lax.broadcasted_iota(I32, (feat, feat), 0) == lax.broadcasted_iota(I32, (feat, feat), 1)
    wout_c[...] = jnp.sum(
        jnp.where(diagonal, jnp.broadcast_to(w_out_ref[...], (feat, feat)), 0.0), axis=1, keepdims=True)
    live = lax.broadcasted_iota(I32, (1, edges), 1) < count_ref[...]
    index_s[0:1, :] = jnp.where(live, center_ref[...], -1)
    index_s[1:2, :] = jnp.where(live, other_ref[...], -1)

    def columns(attr, place):
        emb = nn(emb_t[...], attr)
        emb = emb * sigmoid(emb)
        tail = jnp.zeros((7, place.shape[1]), F32)
        return emb.astype(BF16), jnp.concatenate(list(three_parts(place)) + [tail], axis=0)

    emb, place = columns(own[0:adim], pos)
    tab[0:feat, 0:atoms] = emb
    tab[0:feat, atoms:2 * atoms] = emb
    tab[feat:, 0:atoms] = place.astype(BF16)
    tab[feat:, atoms:2 * atoms] = (-place).astype(BF16)
    shift_cols = atoms

    def part(b):
        return pl.ds(pl.multiple_of(b * block, block), block)

    def own_part(b, _):
        c_row, o_row = index_s[0:1, part(b)], index_s[1:2, part(b)]
        a_c = hits(atoms, c_row, 0)
        one_c[:, part(b)] = a_c
        acc[:, part(b)] = nn(tab[:, 0:2 * atoms], jnp.concatenate([hits(atoms, o_row, 0), a_c], axis=0))
        return 0

    lax.fori_loop(0, nb, own_part, 0)

    moved_at = {}
    for n in range(8):
        rim_copy(n).wait_recv()
        sx, sy = NEAR[n]
        for m, (slot, _) in enumerate(CELLS[sx, sy]):
            cell = got[n, m]
            first = atoms + slot * rim_len
            tail = cell[adim:].astype(F32)
            rows = lax.broadcasted_iota(I32, (3, rim_len), 0)
            shift = jnp.where(rows == 0, float(sx), jnp.where(rows == 1, float(sy), 0.0))
            moved = tail[0:3] + tail[3:6] + shift
            moved_at[slot] = moved
            upper = moved.astype(BF16).astype(F32)
            inner[0:adim, first:first + rim_len] = cell[0:adim]
            inner[adim:, first:first + rim_len] = jnp.concatenate(
                [upper, moved - upper, jnp.zeros((10, rim_len), F32)], axis=0).astype(BF16)
    z_row = z_ref[...]
    picked = nn(inner[...], hits(inner_len, z_row, 0))
    zcell[...] = jnp.concatenate(
        [picked[0:adim + 6], (z_row >> 8).astype(F32), (z_row & 255).astype(F32), picked[adim + 8:]], axis=0).astype(BF16)
    zcopy = pltpu.make_async_remote_copy(
        src_ref=zcell, dst_ref=zgot, send_sem=zsend, recv_sem=zrecv, device_id=partner, device_id_type=MESH)
    zcopy.start()
    emb, place = columns(inner[0:adim, atoms:], jnp.concatenate([moved_at[slot] for slot in range(16)], axis=1))
    tab[0:feat, atoms + shift_cols:inner_len + shift_cols] = emb
    tab[feat:, atoms + shift_cols:inner_len + shift_cols] = place.astype(BF16)

    def cycle_part(b, _):
        o_row = index_s[1:2, part(b)]
        acc[:, part(b)] += nn(
            tab[:, atoms + shift_cols:inner_len + shift_cols], hits(inner_len - atoms, o_row, atoms))
        return 0

    lax.fori_loop(0, nb, cycle_part, 0)

    zcopy.wait_recv()
    cell = zgot[...]
    tail = cell[adim:].astype(F32)
    rows = lax.broadcasted_iota(I32, (3, zlen), 0)
    moved = tail[0:3] + tail[3:6] + jnp.where(rows == 2, (1 - 2 * k).astype(F32), 0.0)
    zlist[0:1, :] = tail[6:7] * 256.0 + tail[7:8]
    emb, place = columns(cell[0:adim], moved)
    tab[0:feat, inner_len + shift_cols:] = emb
    tab[feat:, inner_len + shift_cols:] = place.astype(BF16)

    tens[...] = jnp.zeros_like(tens)

    def geometry(sep):
        sq = jnp.sum(sep * sep, axis=0, keepdims=True)
        inv = lax.rsqrt(sq + 0.25)
        dist = (sq + 0.25) * inv
        env = 1.0 / (1.0 + sq * sq * (1.0 / 16.0))
        radii = 0.5 + 0.4 * lax.broadcasted_iota(I32, (nbas, 1), 0).astype(F32)
        t = (dist - radii) * 2.0
        gauss = jnp.exp(-(t * t))
        return sq, inv, env, t, gauss

    def phase1(b, _):
        o_row = index_s[1:2, part(b)]
        a_c = one_c[:, part(b)]
        m1 = acc[:, part(b)] + nn(tab[:, inner_len + shift_cols:], hits(zlen, o_row, inner_len))
        sep = m1[feat:feat + 3] + m1[feat + 3:feat + 6] + m1[feat + 6:feat + 9]
        sq, inv, env, t, gauss = geometry(sep)
        radial = gauss * env
        r_hi = radial.astype(BF16).astype(F32)
        r_lo = radial - r_hi
        parts = jnp.concatenate([r_hi, r_lo, r_hi, r_lo], axis=0).astype(BF16)
        mixed = m1[0:feat] + nn(wrt[...], parts)
        s = sigmoid(mixed)
        latent = (mixed * s).astype(BF16)
        lat_s[:, part(b)] = latent
        dsilu_s[:, part(b)] = (s * (1.0 + mixed * (1.0 - s))).astype(BF16)
        chan = nn(w_chan_ref[...], latent)
        chan_s[:, part(b)] = chan
        dirs = sep * inv
        x, y, z = dirs[0:1], dirs[1:2], dirs[2:3]
        harm = jnp.concatenate([
            jnp.ones_like(x), x, y, z, ROOT3 * x * y, ROOT3 * y * z, ROOT3 * z * x,
            0.5 * ROOT3 * (x * x - y * y), 0.5 * (3.0 * z * z - 1.0),
            sep, env, jnp.zeros((3, block), F32)], axis=0)
        geo_s[:, part(b)] = harm
        prod = jnp.concatenate([chan] + [chan * harm[m:m + 1] for m in range(1, 9)], axis=0).astype(BF16)
        tens[0:9 * ch] += nt(prod, a_c)
        return 0

    lax.fori_loop(0, nb, phase1, 0)
    tens_b[...] = (0.125 * tens[0:9 * ch]).astype(BF16)
    tens[...] = jnp.zeros_like(tens)

    def phase2(b, _):
        a_c = one_c[:, part(b)]
        harm = geo_s[:, part(b)]
        env = harm[12:13]
        gath = nn(tens_b[...], a_c)
        g = [gath[m * ch:(m + 1) * ch] for m in range(9)]
        h = [harm[m:m + 1] for m in range(9)]
        inv0 = g[0]
        inv1 = g[1] * h[1] + g[2] * h[2] + g[3] * h[3]
        inv2 = g[4] * h[4] + g[5] * h[5] + g[6] * h[6] + g[7] * h[7] + g[8] * h[8]
        invb = jnp.concatenate([inv0, inv1, inv2], axis=0).astype(BF16)
        pre = nn(wcat[...], jnp.concatenate([lat_s[:, part(b)], invb], axis=0))
        s = sigmoid(pre)
        wo = wout_c[...]
        e = jnp.sum(pre * s * wo, axis=0, keepdims=True)
        dpre = (s * (1.0 + pre * (1.0 - s))) * wo * env
        back = nn(wback[...], dpre.astype(BF16))
        acc[0:feat, part(b)] = back[0:feat]
        dinv = [back[feat + l * ch:feat + (l + 1) * ch] for l in range(3)]
        dh = [jnp.sum(dinv[BANDS[m]] * g[m], axis=0, keepdims=True) for m in range(1, 9)]
        en = e * env
        dh_s[:, part(b)] = jnp.concatenate([e] + dh + [jnp.zeros((7, block), F32)], axis=0)
        en_hi = en.astype(BF16).astype(F32)
        prod = jnp.concatenate(
            [dinv[0]] + [dinv[BANDS[m]] * h[m] for m in range(1, 9)] + [en_hi, en - en_hi, jnp.zeros((14, block), F32)],
            axis=0).astype(BF16)
        tens[...] += nt(prod, a_c)
        return 0

    lax.fori_loop(0, nb, phase2, 0)
    energy_ref[...] = tens[9 * ch:9 * ch + 1] + tens[9 * ch + 1:9 * ch + 2]
    tens_b[...] = (0.125 * tens[0:9 * ch]).astype(BF16)
    grad[...] = jnp.zeros_like(grad)
    q_order = list(range(nqc)) + [nqc + slot for slot in SLOT_ORDER] + [nqc + 16]
    nqo = len(q_order)

    def phase3(b, _):
        a_c = one_c[:, part(b)]
        harm = geo_s[:, part(b)]
        gd = nn(tens_b[...], a_c)
        g = [gd[m * ch:(m + 1) * ch] for m in range(9)]
        h = [harm[m:m + 1] for m in range(9)]
        chan = chan_s[:, part(b)]
        dchan = g[0]
        for m in range(1, 9):
            dchan = dchan + g[m] * h[m]
        old = dh_s[:, part(b)]
        d = [None] + [old[m:m + 1] + jnp.sum(chan * g[m], axis=0, keepdims=True) for m in range(1, 9)]
        dlat = acc[0:feat, part(b)] + nn(wchan[...], dchan.astype(BF16))
        dmixed = (dlat * dsilu_s[:, part(b)].astype(F32)).astype(BF16)
        d16 = nn(wr2[...], dmixed)
        drad = d16[0:nbas] + d16[nbas:]
        sep = harm[9:12]
        sq, inv, env, t, gauss = geometry(sep)
        dg = drad * gauss
        d_dist = jnp.sum(dg * t, axis=0, keepdims=True) * (-4.0 * env)
        d_env = jnp.sum(dg, axis=0, keepdims=True) + old[0:1]
        x, y, z = h[1], h[2], h[3]
        dx = d[1] + ROOT3 * (y * d[4] + z * d[6] + x * d[7])
        dy = d[2] + ROOT3 * (x * d[4] + z * d[5] - y * d[7])
        dz = d[3] + ROOT3 * (y * d[5] + x * d[6]) + 3.0 * z * d[8]
        d_dist = d_dist - (dx * x + dy * y + dz * z) * inv
        d_sq = d_dist * (0.5 * inv) - d_env * env * env * sq * 0.125
        dsep = jnp.concatenate([dx, dy, dz], axis=0) * inv + sep * (2.0 * d_sq)
        hi = dsep.astype(BF16).astype(F32)
        d8 = jnp.concatenate([hi, dsep - hi, jnp.zeros((2, block), F32)], axis=0)
        c_row, o_row = index_s[0:1, part(b)], index_s[1:2, part(b)]
        oq, cq = o_row >> 7, c_row >> 7
        lhs = jnp.concatenate(
            [jnp.where(oq == q, d8, 0.0) for q in q_order] + [jnp.where(cq == q, d8, 0.0) for q in range(nqc)],
            axis=0).astype(BF16)
        rhs = jnp.concatenate([hits(128, o_row & 127, 0), hits(128, c_row & 127, 0)], axis=0)
        grad[...] += nt(lhs, rhs)
        return 0

    lax.fori_loop(0, nb, phase3, 0)

    def summed(rows):
        return rows[0:3] + rows[3:6]

    first_of = {}
    rows = nqc
    for n, shift in enumerate(NEAR):
        first_of[n] = rows
        rows += len(CELLS[shift])
    zback[...] = jnp.concatenate(
        [summed(grad[(nqo - 1) * 8:nqo * 8, 0:128]), zlist[0:1, :], jnp.zeros((4, zlen), F32)], axis=0)

    def back_copy(n):
        sx, sy = NEAR[n]
        count = len(CELLS[sx, sy])
        return pltpu.make_async_remote_copy(
            src_ref=grad.at[first_of[n] * 8:(first_of[n] + count) * 8, 0:128], dst_ref=back_got.at[n, 0:count * 8],
            send_sem=bsend.at[n], recv_sem=brecv.at[n], device_id=at(sx, sy, k), device_id_type=MESH)

    def zback_copy(n):
        sx, sy = NEAR[n] if n < 8 else (0, 0)
        return pltpu.make_async_remote_copy(
            src_ref=zback, dst_ref=zback_got.at[n],
            send_sem=zbsend.at[n], recv_sem=zbrecv.at[n], device_id=at(sx, sy, 1 - k), device_id_type=MESH)

    for n in range(9):
        zback_copy(n).start()
        if n < 8:
            back_copy(n).start()

    def parts16(rows):
        return jnp.concatenate(list(three_parts(rows)) + [jnp.zeros((7, rows.shape[1]), F32)], axis=0).astype(BF16)

    def joined(rows):
        return rows[0:3] + rows[3:6] + rows[6:9]

    own_grad = jnp.concatenate(
        [summed(grad[q * 8:(q + 1) * 8, 0:128]) - summed(grad[(nqo + q) * 8:(nqo + q + 1) * 8, 128:256])
         for q in range(nqc)], axis=1)
    rim_back = [jnp.zeros((3, rim_len), F32) for _ in range(8)]
    for n in range(8, -1, -1):
        zback_copy(n).wait_recv()
        message = zback_got[n]
        values = parts16(message[0:3])
        listed = message[3:4].astype(I32)
        if n == 8:
            own_grad = own_grad + joined(nt(values, hits(atoms, listed, 0)))
        else:
            back_copy(n).wait_recv()
            for m, (slot, cell) in enumerate(CELLS[NEAR[n]]):
                from_slab = joined(nt(values, hits(rim_len, listed, atoms + slot * rim_len)))
                rim_back[cell] = rim_back[cell] + summed(back_got[n, m * 8:(m + 1) * 8]) + from_slab
    own_grad = own_grad + joined(nt(parts16(jnp.concatenate(rim_back, axis=1)), rim_hits[...]))
    for c in range(3):
        force_ref[c] = -own_grad[c:c + 1]
    for n in range(8):
        rim_copy(n).wait_send()
        back_copy(n).wait_send()
    for n in range(9):
        zback_copy(n).wait_send()
    zcopy.wait_send()


def per_device(
    positions, attributes, edge_center, edge_other, edge_count, rim_rows, z_rows, w_emb, w_rbf, w_chan, w_lat, w_ten, w_out,
):
    atoms, adim = attributes.shape[3:]
    edges, (feat, ch) = edge_center.shape[3], w_chan.shape
    rim_len, zlen = rim_rows.shape[4], z_rows.shape[3]
    inner_len = atoms + 16 * rim_len
    tbl = inner_len + zlen
    V, D = pltpu.VMEM, pltpu.SemaphoreType.DMA
    spec = pl.BlockSpec(memory_space=pltpu.VMEM)
    energy, forces = pl.pallas_call(
        functools.partial(whole_kernel, block=BLOCK),
        out_shape=(jax.ShapeDtypeStruct((1, atoms), F32), jax.ShapeDtypeStruct((3, 1, atoms), F32)),
        in_specs=[spec] * 13, out_specs=(spec, spec),
        scratch_shapes=[
            V((feat + 16, tbl + atoms), BF16), V((feat + 16, edges), F32), V((atoms, edges), BF16),
            V((feat, edges), BF16), V((feat, edges), BF16), V((ch, edges), F32), V((16, edges), F32), V((16, edges), F32),
            V((2, edges), I32), V((9 * ch + 16, atoms), F32), V((9 * ch, atoms), BF16),
            V(((tbl + atoms) // 128 * 8, 256), F32),
            V((feat, adim), BF16), V((feat, 32), BF16), V((feat, ch), BF16), V((feat, feat + 3 * ch), BF16),
            V((feat + 3 * ch, feat), BF16), V((16, feat), BF16), V((feat, 1), F32), V((atoms, 8 * rim_len), BF16),
            V((8, 3, adim + 16, rim_len), BF16), V((8, 3, adim + 16, rim_len), BF16), V((adim + 16, inner_len), BF16),
            V((adim + 16, zlen), BF16), V((adim + 16, zlen), BF16), V((8, zlen), F32), V((8, zlen), F32),
            V((9, 8, zlen), F32), V((8, 24, rim_len), F32),
            D((8,)), D((8,)), D, D, D((8,)), D((8,)), D((9,)), D((9,))],
        compiler_params=pltpu.CompilerParams(collective_id=0, has_side_effects=True, vmem_limit_bytes=VMEM_LIMIT),
        name="whole",
    )(
        positions.reshape(3, 1, atoms), attributes.reshape(atoms, adim), edge_center.reshape(1, edges),
        edge_other.reshape(1, edges), edge_count.reshape(1, 1), rim_rows.reshape(8, rim_len), z_rows.reshape(1, zlen),
        w_emb, w_rbf, w_chan.T, w_lat, w_ten, w_out.reshape(1, feat))
    return energy.reshape(1, 1, 1, atoms), forces.reshape(1, 1, 1, 3, atoms)


def solution(mesh):
    spread = P("gx", "gy", "gz")
    return jax.shard_map(
        per_device,
        mesh=mesh,
        in_specs=(spread,) * 7 + (P(),) * 6,
        out_specs=(spread, spread),
        check_vma=False,
    )
```

```python
import functools

import jax
import jax.numpy as jnp
from jax import lax
from jax.experimental import pallas as pl
from jax.experimental.pallas import tpu as pltpu
from jax.sharding import PartitionSpec as P

F32, BF16, I32 = jnp.float32, jnp.bfloat16, jnp.int32
ROOT3 = 3.0 ** 0.5
BANDS = (0, 1, 1, 1, 2, 2, 2, 2, 2)
BLOCK = 2048
VMEM_LIMIT = 62 << 20
MESH = pl.DeviceIdType.MESH
RIM_CELLS = [(0, 0), (0, 1), (0, 2), (1, 0), (1, 2), (2, 0), (2, 1), (2, 2)]


def source_of(position):
    if position == 0:
        return (-1, 2)
    if position == 4:
        return (1, 0)
    return (0, position - 1)


NEAR = [(0, 1), (0, -1), (1, 1), (1, -1), (-1, 1), (-1, -1), (1, 0), (-1, 0)]
CELLS = {shift: [] for shift in NEAR}
slots = 0
for row in range(5):
    for column in range(5):
        if row in (0, 4) or column in (0, 4):
            sx, ra = source_of(row)
            sy, rb = source_of(column)
            CELLS[sx, sy].append((slots, RIM_CELLS.index((ra, rb))))
            slots += 1
SLOT_ORDER = [slot for shift in NEAR for slot, _ in CELLS[shift]]
EARLY, LATE = [(1, 3), (12, 3)], [(0, 1), (4, 8), (15, 1)]


def nt(a, b):
    return lax.dot_general(a, b, (((1,), (1,)), ((), ())), preferred_element_type=F32)


def nn(a, b):
    return jnp.dot(a, b, preferred_element_type=F32)


def turned(w, unit):
    return lax.dot_general(w, unit, (((0,), (0,)), ((), ())), preferred_element_type=F32).astype(BF16)


def sigmoid(x):
    return 0.5 * jnp.tanh(0.5 * x) + 0.5


def eye(n):
    rows = lax.broadcasted_iota(I32, (n, n), 0)
    cols = lax.broadcasted_iota(I32, (n, n), 1)
    return jnp.where(rows == cols, 1.0, 0.0).astype(BF16)


def three_parts(v):
    upper = v.astype(BF16).astype(F32)
    rest = v - upper
    middle = rest.astype(BF16).astype(F32)
    return upper, middle, rest - middle


def hits(rows, index_row, offset):
    width = index_row.shape[1]
    ids = lax.broadcasted_iota(jnp.int16, (rows, width), 0)
    wanted = jnp.broadcast_to((index_row - offset).astype(jnp.int16), (rows, width))
    return jnp.where(ids == wanted, jnp.ones((), BF16), jnp.zeros((), BF16))


def whole_kernel(*refs, block):
    sources, out_ref = refs[:13], refs[13]
    held, rest = refs[14:27], refs[27:]
    (pos_ref, attr_ref, rim_ref, z_ref, center_ref, other_ref, count_ref,
     w_emb_ref, w_rbf_ref, w_chan_ref, w_lat_ref, w_ten_ref, w_out_ref) = held
    (in_sem, tab, acc, one_c, lat_s, dsilu_s, chan_s, geo_s, dh_s, index_s, tens, tens_b, grad,
     emb_t, wrt, wchan, wcat, wback, wr2, wout_c, rim_hits, zhits,
     cells, got, inner, zcell, zgot, zback_got, back_got,
     send_sem, recv_sem, zsend, zrecv, bsend, brecv, zbsend, zbrecv) = rest

    def fetch(n):
        return pltpu.make_async_copy(sources[n], held[n], in_sem.at[n])

    adim, feat = w_emb_ref.shape
    ch, nbas = w_chan_ref.shape[0], w_rbf_ref.shape[0]
    atoms, edges = attr_ref.shape[0], center_ref.shape[1]
    rim_len, zlen = rim_ref.shape[1], z_ref.shape[1]
    inner_len = atoms + 16 * rim_len
    tbl = inner_len + zlen
    nb = edges // block
    nqc = atoms // 128

    i, j, k = (lax.axis_index(name) for name in ("gx", "gy", "gz"))
    nx, ny = lax.axis_size("gx"), lax.axis_size("gy")

    def at(sx, sy, side):
        return (lax.rem(i + (sx + nx), nx), lax.rem(j + (sy + ny), ny), side)

    partner = (i, j, 1 - k)
    barrier = pltpu.get_barrier_semaphore()
    for sx, sy in NEAR:
        pl.semaphore_signal(barrier, inc=1, device_id=at(sx, sy, k), device_id_type=MESH)
        pl.semaphore_signal(barrier, inc=1, device_id=at(sx, sy, 1 - k), device_id_type=MESH)
    pl.semaphore_signal(barrier, inc=1, device_id=partner, device_id_type=MESH)
    for n in range(13):
        fetch(n).start()
    for n in range(4):
        fetch(n).wait()

    pos = jnp.concatenate([pos_ref[0], pos_ref[1], pos_ref[2]], axis=0)
    upper = pos.astype(BF16).astype(F32)
    own = jnp.concatenate(
        [nt(eye(adim), attr_ref[...]), upper, pos - upper, jnp.zeros((10, atoms), F32)], axis=0).astype(BF16)
    inner[:, 0:atoms] = own
    rim_row = jnp.concatenate([rim_ref[c:c + 1, :] for c in range(8)], axis=1)
    rim_hits[:, 0:8 * rim_len] = hits(atoms, rim_row, 0)
    z_row = z_ref[...]
    z_rows = [(z_row >> 8).astype(F32), (z_row & 255).astype(F32)]
    packed = nn(own, rim_hits[:, 0:8 * rim_len])
    for n, shift in enumerate(NEAR):
        for m, (_, cell) in enumerate(CELLS[shift]):
            rows = packed[:, cell * rim_len:(cell + 1) * rim_len]
            cells[n, m] = jnp.concatenate([rows[0:adim + 6]] + z_rows + [rows[adim + 8:]], axis=0).astype(BF16)
    pl.semaphore_wait(barrier, 17)

    def rim_copy(n):
        sx, sy = NEAR[n]
        count = len(CELLS[sx, sy])
        return pltpu.make_async_remote_copy(
            src_ref=cells.at[n, 0:count], dst_ref=got.at[n, 0:count], send_sem=send_sem.at[n], recv_sem=recv_sem.at[n],
            device_id=at(-sx, -sy, k), device_id_type=MESH)

    for n in range(8):
        rim_copy(n).start()

    for n in range(4, 13):
        fetch(n).wait()
    big_eye = eye(feat)
    emb_t[...] = turned(w_emb_ref[...], eye(adim))
    wchan[...] = turned(w_chan_ref[...], eye(ch))
    wcat[:, 0:feat] = turned(w_lat_ref[...], big_eye)
    wcat[:, feat:] = turned(w_ten_ref[...], eye(3 * ch))
    wback[0:feat, :] = w_lat_ref[...]
    wback[feat:, :] = w_ten_ref[...]
    rb = w_rbf_ref[...]
    rb_hi = rb.astype(BF16).astype(F32)
    rb_lo = rb - rb_hi
    wr2[...] = jnp.concatenate([rb_hi, rb_lo], axis=0).astype(BF16)
    wrt[...] = nt(big_eye, jnp.concatenate([rb_hi, rb_hi, rb_lo, rb_lo], axis=0).astype(BF16)).astype(BF16)
    diagonal = lax.broadcasted_iota(I32, (feat, feat), 0) == lax.broadcasted_iota(I32, (feat, feat), 1)
    wout_c[...] = jnp.sum(
        jnp.where(diagonal, jnp.broadcast_to(w_out_ref[...], (feat, feat)), 0.0), axis=1, keepdims=True)
    live = lax.broadcasted_iota(I32, (1, edges), 1) < count_ref[...]
    index_s[0:1, :] = jnp.where(live, center_ref[...], -1)
    index_s[1:2, :] = jnp.where(live, other_ref[...], -1)

    def columns(attr, place):
        emb = nn(emb_t[...], attr)
        emb = emb * sigmoid(emb)
        tail = jnp.zeros((7, place.shape[1]), F32)
        return emb.astype(BF16), jnp.concatenate(list(three_parts(place)) + [tail], axis=0)

    emb, place = columns(own[0:adim], pos)
    tab[0:feat, 0:atoms] = emb
    tab[0:feat, atoms:2 * atoms] = emb
    tab[feat:, 0:atoms] = place.astype(BF16)
    tab[feat:, atoms:2 * atoms] = (-place).astype(BF16)
    shift_cols = atoms

    def part(b):
        return pl.ds(pl.multiple_of(b * block, block), block)

    def own_part(b, _):
        c_row, o_row = index_s[0:1, part(b)], index_s[1:2, part(b)]
        a_c = hits(atoms, c_row, 0)
        one_c[:, part(b)] = a_c
        acc[:, part(b)] = nn(tab[:, 0:2 * atoms], jnp.concatenate([hits(atoms, o_row, 0), a_c], axis=0))
        return 0

    lax.fori_loop(0, nb, own_part, 0)

    rim_hits[:, 8 * rim_len:] = hits(atoms, z_row, 0)
    moved_at = {}
    columns_of = [None] * 8

    def take(n):
        rim_copy(n).wait_recv()
        sx, sy = NEAR[n]
        for m, (slot, _) in enumerate(CELLS[sx, sy]):
            cell = got[n, m]
            first = atoms + slot * rim_len
            tail = cell[adim:].astype(F32)
            rows = lax.broadcasted_iota(I32, (3, rim_len), 0)
            shift = jnp.where(rows == 0, float(sx), jnp.where(rows == 1, float(sy), 0.0))
            moved = tail[0:3] + tail[3:6] + shift
            moved_at[slot] = moved
            upper = moved.astype(BF16).astype(F32)
            inner[0:adim, first:first + rim_len] = cell[0:adim]
            inner[adim:, first:first + rim_len] = jnp.concatenate(
                [upper, moved - upper, jnp.zeros((10, rim_len), F32)], axis=0).astype(BF16)
        listed = (got[n, 0][adim + 6:adim + 7].astype(F32) * 256.0 + got[n, 0][adim + 7:adim + 8].astype(F32)).astype(I32)
        column = jnp.full_like(listed, -1)
        for slot, cell in CELLS[-sx, -sy]:
            row = listed - (atoms + slot * rim_len)
            column = jnp.where((row >= 0) & (row < rim_len), row + cell * rim_len, column)
        columns_of[NEAR.index((-sx, -sy))] = column

    def fill(runs, first):
        attr = jnp.concatenate(
            [inner[0:adim, atoms + r * rim_len:atoms + (r + c) * rim_len] for r, c in runs], axis=1)
        emb, place = columns(attr, jnp.concatenate([moved_at[r + q] for r, c in runs for q in range(c)], axis=1))
        width = emb.shape[1]
        tab[0:feat, first:first + width] = emb
        tab[feat:, first:first + width] = place.astype(BF16)
        return width

    def add_part(runs, first, width):
        def step(b, _):
            o_row = index_s[1:2, part(b)]
            picks = jnp.concatenate([hits(c * rim_len, o_row, atoms + r * rim_len) for r, c in runs], axis=0)
            acc[:, part(b)] += nn(tab[:, first:first + width], picks)
            return 0

        lax.fori_loop(0, nb, step, 0)

    for n in (6, 7):
        take(n)
    early = fill(EARLY, 2 * atoms)
    add_part(EARLY, 2 * atoms, early)
    for n in range(6):
        take(n)
    zcell[...] = nn(inner[...], hits(inner_len, z_row, 0)).astype(BF16)
    zcopy = pltpu.make_async_remote_copy(
        src_ref=zcell, dst_ref=zgot, send_sem=zsend, recv_sem=zrecv, device_id=partner, device_id_type=MESH)
    zcopy.start()
    late = fill(LATE, 2 * atoms + early)
    add_part(LATE, 2 * atoms + early, late)
    zhits[...] = hits(8 * rim_len, jnp.concatenate(columns_of, axis=1), 0)

    zcopy.wait_recv()
    cell = zgot[...]
    tail = cell[adim:].astype(F32)
    rows = lax.broadcasted_iota(I32, (3, zlen), 0)
    moved = tail[0:3] + tail[3:6] + jnp.where(rows == 2, (1 - 2 * k).astype(F32), 0.0)
    emb, place = columns(cell[0:adim], moved)
    tab[0:feat, inner_len + shift_cols:] = emb
    tab[feat:, inner_len + shift_cols:] = place.astype(BF16)

    tens[...] = jnp.zeros_like(tens)

    def geometry(sep):
        sq = jnp.sum(sep * sep, axis=0, keepdims=True)
        inv = lax.rsqrt(sq + 0.25)
        dist = (sq + 0.25) * inv
        env = 1.0 / (1.0 + sq * sq * (1.0 / 16.0))
        radii = 0.5 + 0.4 * lax.broadcasted_iota(I32, (nbas, 1), 0).astype(F32)
        t = (dist - radii) * 2.0
        gauss = jnp.exp(-(t * t))
        return sq, inv, env, t, gauss

    def phase1(b, _):
        o_row = index_s[1:2, part(b)]
        a_c = one_c[:, part(b)]
        m1 = acc[:, part(b)] + nn(tab[:, inner_len + shift_cols:], hits(zlen, o_row, inner_len))
        sep = m1[feat:feat + 3] + m1[feat + 3:feat + 6] + m1[feat + 6:feat + 9]
        sq, inv, env, t, gauss = geometry(sep)
        radial = gauss * env
        r_hi = radial.astype(BF16).astype(F32)
        r_lo = radial - r_hi
        parts = jnp.concatenate([r_hi, r_lo, r_hi, r_lo], axis=0).astype(BF16)
        mixed = m1[0:feat] + nn(wrt[...], parts)
        s = sigmoid(mixed)
        latent = (mixed * s).astype(BF16)
        lat_s[:, part(b)] = latent
        dsilu_s[:, part(b)] = (s * (1.0 + mixed * (1.0 - s))).astype(BF16)
        chan = nn(w_chan_ref[...], latent)
        chan_s[:, part(b)] = chan
        dirs = sep * inv
        x, y, z = dirs[0:1], dirs[1:2], dirs[2:3]
        harm = jnp.concatenate([
            jnp.ones_like(x), x, y, z, ROOT3 * x * y, ROOT3 * y * z, ROOT3 * z * x,
            0.5 * ROOT3 * (x * x - y * y), 0.5 * (3.0 * z * z - 1.0),
            sep, env, jnp.zeros((3, block), F32)], axis=0)
        geo_s[:, part(b)] = harm
        prod = jnp.concatenate([chan] + [chan * harm[m:m + 1] for m in range(1, 9)], axis=0).astype(BF16)
        tens[0:9 * ch] += nt(prod, a_c)
        return 0

    lax.fori_loop(0, nb, phase1, 0)
    tens_b[...] = (0.125 * tens[0:9 * ch]).astype(BF16)
    tens[...] = jnp.zeros_like(tens)

    def phase2(b, _):
        a_c = one_c[:, part(b)]
        harm = geo_s[:, part(b)]
        env = harm[12:13]
        gath = nn(tens_b[...], a_c)
        g = [gath[m * ch:(m + 1) * ch] for m in range(9)]
        h = [harm[m:m + 1] for m in range(9)]
        inv0 = g[0]
        inv1 = g[1] * h[1] + g[2] * h[2] + g[3] * h[3]
        inv2 = g[4] * h[4] + g[5] * h[5] + g[6] * h[6] + g[7] * h[7] + g[8] * h[8]
        invb = jnp.concatenate([inv0, inv1, inv2], axis=0).astype(BF16)
        pre = nn(wcat[...], jnp.concatenate([lat_s[:, part(b)], invb], axis=0))
        s = sigmoid(pre)
        wo = wout_c[...]
        e = jnp.sum(pre * s * wo, axis=0, keepdims=True)
        dpre = (s * (1.0 + pre * (1.0 - s))) * wo * env
        back = nn(wback[...], dpre.astype(BF16))
        acc[0:feat, part(b)] = back[0:feat]
        dinv = [back[feat + l * ch:feat + (l + 1) * ch] for l in range(3)]
        dh = [jnp.sum(dinv[BANDS[m]] * g[m], axis=0, keepdims=True) for m in range(1, 9)]
        en = e * env
        dh_s[:, part(b)] = jnp.concatenate([e] + dh + [jnp.zeros((7, block), F32)], axis=0)
        en_hi = en.astype(BF16).astype(F32)
        prod = jnp.concatenate(
            [dinv[0]] + [dinv[BANDS[m]] * h[m] for m in range(1, 9)] + [en_hi, en - en_hi, jnp.zeros((14, block), F32)],
            axis=0).astype(BF16)
        tens[...] += nt(prod, a_c)
        return 0

    lax.fori_loop(0, nb, phase2, 0)
    out_ref[3] = -(tens[9 * ch:9 * ch + 1] + tens[9 * ch + 1:9 * ch + 2])
    tens_b[...] = (0.125 * tens[0:9 * ch]).astype(BF16)
    grad[...] = jnp.zeros_like(grad)
    q_order = list(range(nqc)) + [nqc + slot for slot in SLOT_ORDER] + [nqc + 16]
    nqo = len(q_order)

    def phase3(b, _):
        a_c = one_c[:, part(b)]
        harm = geo_s[:, part(b)]
        gd = nn(tens_b[...], a_c)
        g = [gd[m * ch:(m + 1) * ch] for m in range(9)]
        h = [harm[m:m + 1] for m in range(9)]
        chan = chan_s[:, part(b)]
        dchan = g[0]
        for m in range(1, 9):
            dchan = dchan + g[m] * h[m]
        old = dh_s[:, part(b)]
        d = [None] + [old[m:m + 1] + jnp.sum(chan * g[m], axis=0, keepdims=True) for m in range(1, 9)]
        dlat = acc[0:feat, part(b)] + nn(wchan[...], dchan.astype(BF16))
        dmixed = (dlat * dsilu_s[:, part(b)].astype(F32)).astype(BF16)
        d16 = nn(wr2[...], dmixed)
        drad = d16[0:nbas] + d16[nbas:]
        sep = harm[9:12]
        sq, inv, env, t, gauss = geometry(sep)
        dg = drad * gauss
        d_dist = jnp.sum(dg * t, axis=0, keepdims=True) * (-4.0 * env)
        d_env = jnp.sum(dg, axis=0, keepdims=True) + old[0:1]
        x, y, z = h[1], h[2], h[3]
        dx = d[1] + ROOT3 * (y * d[4] + z * d[6] + x * d[7])
        dy = d[2] + ROOT3 * (x * d[4] + z * d[5] - y * d[7])
        dz = d[3] + ROOT3 * (y * d[5] + x * d[6]) + 3.0 * z * d[8]
        d_dist = d_dist - (dx * x + dy * y + dz * z) * inv
        d_sq = d_dist * (0.5 * inv) - d_env * env * env * sq * 0.125
        dsep = jnp.concatenate([dx, dy, dz], axis=0) * inv + sep * (2.0 * d_sq)
        hi = dsep.astype(BF16).astype(F32)
        d8 = jnp.concatenate([hi, dsep - hi, jnp.zeros((2, block), F32)], axis=0)
        c_row, o_row = index_s[0:1, part(b)], index_s[1:2, part(b)]
        oq, cq = o_row >> 7, c_row >> 7
        lhs = jnp.concatenate(
            [jnp.where(oq == q, d8, 0.0) for q in q_order] + [jnp.where(cq == q, d8, 0.0) for q in range(nqc)],
            axis=0).astype(BF16)
        rhs = jnp.concatenate([hits(128, o_row & 127, 0), hits(128, c_row & 127, 0)], axis=0)
        grad[...] += nt(lhs, rhs)
        return 0

    lax.fori_loop(0, nb, phase3, 0)

    def summed(rows):
        return rows[0:3] + rows[3:6]

    first_of = {}
    rows = nqc
    for n, shift in enumerate(NEAR):
        first_of[n] = rows
        rows += len(CELLS[shift])
    def back_copy(n):
        sx, sy = NEAR[n]
        count = len(CELLS[sx, sy])
        return pltpu.make_async_remote_copy(
            src_ref=grad.at[first_of[n] * 8:(first_of[n] + count) * 8, 0:128], dst_ref=back_got.at[n, 0:count * 8],
            send_sem=bsend.at[n], recv_sem=brecv.at[n], device_id=at(sx, sy, k), device_id_type=MESH)

    def zback_copy(n):
        sx, sy = NEAR[n] if n < 8 else (0, 0)
        return pltpu.make_async_remote_copy(
            src_ref=grad.at[(nqo - 1) * 8:nqo * 8, 0:128], dst_ref=zback_got.at[n],
            send_sem=zbsend.at[n], recv_sem=zbrecv.at[n], device_id=at(sx, sy, 1 - k), device_id_type=MESH)

    for n in range(9):
        zback_copy(n).start()
        if n < 8:
            back_copy(n).start()

    def parts16(rows):
        return jnp.concatenate(list(three_parts(rows)) + [jnp.zeros((7, rows.shape[1]), F32)], axis=0).astype(BF16)

    def joined(rows):
        return rows[0:3] + rows[3:6] + rows[6:9]

    own_grad = jnp.concatenate(
        [summed(grad[q * 8:(q + 1) * 8, 0:128]) - summed(grad[(nqo + q) * 8:(nqo + q + 1) * 8, 128:256])
         for q in range(nqc)], axis=1)
    for n in range(9):
        zback_copy(n).wait_recv()
    slab_back = parts16(jnp.concatenate([summed(zback_got[n]) for n in range(8)], axis=1))
    rim_back = joined(nt(slab_back, zhits[...]))
    added = [jnp.zeros((3, rim_len), F32) for _ in range(8)]
    for n in range(8):
        back_copy(n).wait_recv()
        for m, (_, cell) in enumerate(CELLS[NEAR[n]]):
            added[cell] = added[cell] + summed(back_got[n, m * 8:(m + 1) * 8])
    rim_back = rim_back + jnp.concatenate(added, axis=1)
    last = jnp.concatenate([rim_back, summed(zback_got[8])], axis=1)
    own_grad = own_grad + joined(nt(parts16(last), rim_hits[...]))
    for c in range(3):
        out_ref[c] = own_grad[c:c + 1]
    for n in range(8):
        rim_copy(n).wait_send()
        back_copy(n).wait_send()
    for n in range(9):
        zback_copy(n).wait_send()
    zcopy.wait_send()


def per_device(
    positions, attributes, edge_center, edge_other, edge_count, rim_rows, z_rows, w_emb, w_rbf, w_chan, w_lat, w_ten, w_out,
):
    atoms, adim = attributes.shape[3:]
    edges, (feat, ch) = edge_center.shape[3], w_chan.shape
    rim_len, zlen = rim_rows.shape[4], z_rows.shape[3]
    inner_len = atoms + 16 * rim_len
    tbl = inner_len + zlen
    V, D = pltpu.VMEM, pltpu.SemaphoreType.DMA
    arrays = (
        positions.reshape(3, 1, atoms), attributes.reshape(atoms, adim), rim_rows.reshape(8, rim_len),
        z_rows.reshape(1, zlen), edge_center.reshape(1, edges), edge_other.reshape(1, edges), edge_count.reshape(1, 1),
        w_emb, w_rbf, w_chan.T, w_lat, w_ten, w_out.reshape(1, feat))
    result = pl.pallas_call(
        functools.partial(whole_kernel, block=BLOCK),
        out_shape=jax.ShapeDtypeStruct((4, 1, atoms), F32),
        in_specs=[pl.BlockSpec(memory_space=pl.ANY)] * 13, out_specs=pl.BlockSpec(memory_space=pltpu.VMEM),
        scratch_shapes=[V(array.shape, array.dtype) for array in arrays] + [D((13,))] + [
            V((feat + 16, tbl + atoms), BF16), V((feat + 16, edges), F32), V((atoms, edges), BF16),
            V((feat, edges), BF16), V((feat, edges), BF16), V((ch, edges), F32), V((16, edges), F32), V((16, edges), F32),
            V((2, edges), I32), V((9 * ch + 16, atoms), F32), V((9 * ch, atoms), BF16),
            V(((tbl + atoms) // 128 * 8, 256), F32),
            V((feat, adim), BF16), V((feat, 32), BF16), V((feat, ch), BF16), V((feat, feat + 3 * ch), BF16),
            V((feat + 3 * ch, feat), BF16), V((16, feat), BF16), V((feat, 1), F32), V((atoms, 8 * rim_len + zlen), BF16),
            V((8 * rim_len, 8 * zlen), BF16),
            V((8, 3, adim + 16, rim_len), BF16), V((8, 3, adim + 16, rim_len), BF16), V((adim + 16, inner_len), BF16),
            V((adim + 16, zlen), BF16), V((adim + 16, zlen), BF16), V((9, 8, zlen), F32), V((8, 24, rim_len), F32),
            D((8,)), D((8,)), D, D, D((8,)), D((8,)), D((9,)), D((9,))],
        compiler_params=pltpu.CompilerParams(collective_id=0, has_side_effects=True, vmem_limit_bytes=VMEM_LIMIT),
        name="whole",
    )(*arrays)
    return -result[3].reshape(1, 1, 1, atoms), -result[0:3].reshape(1, 1, 1, 3, atoms)


def solution(mesh):
    spread = P("gx", "gy", "gz")
    return jax.shard_map(
        per_device,
        mesh=mesh,
        in_specs=(spread,) * 7 + (P(),) * 6,
        out_specs=(spread, spread),
        check_vma=False,
    )
```

```python
import functools

import jax
import jax.numpy as jnp
from jax import lax
from jax.experimental import pallas as pl
from jax.experimental.pallas import tpu as pltpu
from jax.sharding import PartitionSpec as P

F32, BF16, I32 = jnp.float32, jnp.bfloat16, jnp.int32
ROOT3 = 3.0 ** 0.5
BANDS = (0, 1, 1, 1, 2, 2, 2, 2, 2)
BLOCK = 2048
VMEM_LIMIT = 62 << 20
MESH = pl.DeviceIdType.MESH
RIM_CELLS = [(0, 0), (0, 1), (0, 2), (1, 0), (1, 2), (2, 0), (2, 1), (2, 2)]


def source_of(position):
    if position == 0:
        return (-1, 2)
    if position == 4:
        return (1, 0)
    return (0, position - 1)


NEAR = [(0, 1), (0, -1), (1, 1), (1, -1), (-1, 1), (-1, -1), (1, 0), (-1, 0)]
CELLS = {shift: [] for shift in NEAR}
slots = 0
for row in range(5):
    for column in range(5):
        if row in (0, 4) or column in (0, 4):
            sx, ra = source_of(row)
            sy, rb = source_of(column)
            CELLS[sx, sy].append((slots, RIM_CELLS.index((ra, rb))))
            slots += 1
SLOT_ORDER = [slot for shift in NEAR for slot, _ in CELLS[shift]]
EARLY, LATE = [(1, 3), (12, 3)], [(0, 1), (4, 8), (15, 1)]


def nt(a, b):
    return lax.dot_general(a, b, (((1,), (1,)), ((), ())), preferred_element_type=F32)


def nn(a, b):
    return jnp.dot(a, b, preferred_element_type=F32)


def turned(w, unit):
    return lax.dot_general(w, unit, (((0,), (0,)), ((), ())), preferred_element_type=F32).astype(BF16)


def sigmoid(x):
    return 0.5 * jnp.tanh(0.5 * x) + 0.5


def eye(n):
    rows = lax.broadcasted_iota(I32, (n, n), 0)
    cols = lax.broadcasted_iota(I32, (n, n), 1)
    return jnp.where(rows == cols, 1.0, 0.0).astype(BF16)


def three_parts(v):
    upper = v.astype(BF16).astype(F32)
    rest = v - upper
    middle = rest.astype(BF16).astype(F32)
    return upper, middle, rest - middle


def hits(rows, index_row, offset):
    width = index_row.shape[1]
    ids = lax.broadcasted_iota(jnp.int16, (rows, width), 0)
    wanted = jnp.broadcast_to((index_row - offset).astype(jnp.int16), (rows, width))
    return jnp.where(ids == wanted, jnp.ones((), BF16), jnp.zeros((), BF16))


def whole_kernel(*refs, block):
    sources, out_ref = refs[:13], refs[13]
    held, rest = refs[14:27], refs[27:]
    (pos_ref, attr_ref, rim_ref, z_ref, center_ref, other_ref, count_ref,
     w_emb_ref, w_rbf_ref, w_chan_ref, w_lat_ref, w_ten_ref, w_out_ref) = held
    (in_sem, tab, acc, one_c, lat_s, dsilu_s, chan_s, geo_s, dh_s, index_s, tens, tens_b, grad,
     emb_t, wrt, wchan, wcat, wback, wr2, wout_c, rim_hits, zhits,
     cells, got, inner, zcell, zgot, zback_got, back_got,
     send_sem, recv_sem, zsend, zrecv, bsend, brecv, zbsend, zbrecv) = rest

    def fetch(n):
        return pltpu.make_async_copy(sources[n], held[n], in_sem.at[n])

    adim, feat = w_emb_ref.shape
    ch, nbas = w_chan_ref.shape[0], w_rbf_ref.shape[0]
    atoms, edges = attr_ref.shape[0], center_ref.shape[1]
    rim_len, zlen = rim_ref.shape[1], z_ref.shape[1]
    inner_len = atoms + 16 * rim_len
    tbl = inner_len + zlen
    nb = edges // block
    nqc = atoms // 128

    i, j, k = (lax.axis_index(name) for name in ("gx", "gy", "gz"))
    nx, ny = lax.axis_size("gx"), lax.axis_size("gy")

    def at(sx, sy, side):
        return (lax.rem(i + (sx + nx), nx), lax.rem(j + (sy + ny), ny), side)

    partner = (i, j, 1 - k)
    barrier = pltpu.get_barrier_semaphore()
    for sx, sy in NEAR:
        pl.semaphore_signal(barrier, inc=1, device_id=at(sx, sy, k), device_id_type=MESH)
        pl.semaphore_signal(barrier, inc=1, device_id=at(sx, sy, 1 - k), device_id_type=MESH)
    pl.semaphore_signal(barrier, inc=1, device_id=partner, device_id_type=MESH)
    for n in range(13):
        fetch(n).start()
    for n in range(4):
        fetch(n).wait()

    pos = jnp.concatenate([pos_ref[0], pos_ref[1], pos_ref[2]], axis=0)
    upper = pos.astype(BF16).astype(F32)
    own = jnp.concatenate(
        [nt(eye(adim), attr_ref[...]), upper, pos - upper, jnp.zeros((10, atoms), F32)], axis=0).astype(BF16)
    inner[:, 0:atoms] = own
    rim_row = jnp.concatenate([rim_ref[c:c + 1, :] for c in range(8)], axis=1)
    rim_hits[:, 0:8 * rim_len] = hits(atoms, rim_row, 0)
    z_row = z_ref[...]
    z_rows = [(z_row >> 8).astype(F32), (z_row & 255).astype(F32)]
    packed = nn(own, rim_hits[:, 0:8 * rim_len])
    for n, shift in enumerate(NEAR):
        for m, (_, cell) in enumerate(CELLS[shift]):
            rows = packed[:, cell * rim_len:(cell + 1) * rim_len]
            cells[n, m] = jnp.concatenate([rows[0:adim + 6]] + z_rows + [rows[adim + 8:]], axis=0).astype(BF16)
    pl.semaphore_wait(barrier, 17)

    def rim_copy(n):
        sx, sy = NEAR[n]
        count = len(CELLS[sx, sy])
        return pltpu.make_async_remote_copy(
            src_ref=cells.at[n, 0:count], dst_ref=got.at[n, 0:count], send_sem=send_sem.at[n], recv_sem=recv_sem.at[n],
            device_id=at(-sx, -sy, k), device_id_type=MESH)

    for n in range(8):
        rim_copy(n).start()

    for n in range(4, 13):
        fetch(n).wait()
    big_eye = eye(feat)
    emb_t[...] = turned(w_emb_ref[...], eye(adim))
    wchan[...] = turned(w_chan_ref[...], eye(ch))
    wcat[:, 0:feat] = turned(w_lat_ref[...], big_eye)
    wcat[:, feat:] = turned(w_ten_ref[...], eye(3 * ch))
    wback[0:feat, :] = w_lat_ref[...]
    wback[feat:, :] = w_ten_ref[...]
    rb = w_rbf_ref[...]
    rb_hi = rb.astype(BF16).astype(F32)
    rb_lo = rb - rb_hi
    wr2[...] = jnp.concatenate([rb_hi, rb_lo], axis=0).astype(BF16)
    wrt[:, zlen:] = nt(big_eye, jnp.concatenate([rb_hi, rb_hi, rb_lo, rb_lo], axis=0).astype(BF16)).astype(BF16)
    diagonal = lax.broadcasted_iota(I32, (feat, feat), 0) == lax.broadcasted_iota(I32, (feat, feat), 1)
    wout_c[...] = jnp.sum(
        jnp.where(diagonal, jnp.broadcast_to(w_out_ref[...], (feat, feat)), 0.0), axis=1, keepdims=True)
    live = lax.broadcasted_iota(I32, (1, edges), 1) < count_ref[...]
    index_s[0:1, :] = jnp.where(live, center_ref[...], -1)
    index_s[1:2, :] = jnp.where(live, other_ref[...], -1)

    def columns(attr, place):
        emb = nn(emb_t[...], attr)
        emb = emb * sigmoid(emb)
        tail = jnp.zeros((7, place.shape[1]), F32)
        return emb.astype(BF16), jnp.concatenate(list(three_parts(place)) + [tail], axis=0)

    emb, place = columns(own[0:adim], pos)
    tab[0:feat, 0:atoms] = emb
    tab[0:feat, atoms:2 * atoms] = emb
    tab[feat:, 0:atoms] = place.astype(BF16)
    tab[feat:, atoms:2 * atoms] = (-place).astype(BF16)
    shift_cols = atoms

    def part(b):
        return pl.ds(pl.multiple_of(b * block, block), block)

    def own_part(b, _):
        c_row, o_row = index_s[0:1, part(b)], index_s[1:2, part(b)]
        a_c = hits(atoms, c_row, 0)
        one_c[:, part(b)] = a_c
        acc[:, part(b)] = nn(tab[:, 0:2 * atoms], jnp.concatenate([hits(atoms, o_row, 0), a_c], axis=0))
        return 0

    lax.fori_loop(0, nb, own_part, 0)

    rim_hits[:, 8 * rim_len:] = hits(atoms, z_row, 0)
    moved_at = {}
    columns_of = [None] * 8

    def take(n):
        rim_copy(n).wait_recv()
        sx, sy = NEAR[n]
        for m, (slot, _) in enumerate(CELLS[sx, sy]):
            cell = got[n, m]
            first = atoms + slot * rim_len
            tail = cell[adim:].astype(F32)
            rows = lax.broadcasted_iota(I32, (3, rim_len), 0)
            shift = jnp.where(rows == 0, float(sx), jnp.where(rows == 1, float(sy), 0.0))
            moved = tail[0:3] + tail[3:6] + shift
            moved_at[slot] = moved
            upper = moved.astype(BF16).astype(F32)
            inner[0:adim, first:first + rim_len] = cell[0:adim]
            inner[adim:, first:first + rim_len] = jnp.concatenate(
                [upper, moved - upper, jnp.zeros((10, rim_len), F32)], axis=0).astype(BF16)
        listed = (got[n, 0][adim + 6:adim + 7].astype(F32) * 256.0 + got[n, 0][adim + 7:adim + 8].astype(F32)).astype(I32)
        column = jnp.full_like(listed, -1)
        for slot, cell in CELLS[-sx, -sy]:
            row = listed - (atoms + slot * rim_len)
            column = jnp.where((row >= 0) & (row < rim_len), row + cell * rim_len, column)
        columns_of[NEAR.index((-sx, -sy))] = column

    def fill(runs, first):
        attr = jnp.concatenate(
            [inner[0:adim, atoms + r * rim_len:atoms + (r + c) * rim_len] for r, c in runs], axis=1)
        emb, place = columns(attr, jnp.concatenate([moved_at[r + q] for r, c in runs for q in range(c)], axis=1))
        width = emb.shape[1]
        tab[0:feat, first:first + width] = emb
        tab[feat:, first:first + width] = place.astype(BF16)
        return width

    def add_part(runs, first, width):
        def step(b, _):
            o_row = index_s[1:2, part(b)]
            picks = jnp.concatenate([hits(c * rim_len, o_row, atoms + r * rim_len) for r, c in runs], axis=0)
            acc[:, part(b)] += nn(tab[:, first:first + width], picks)
            return 0

        lax.fori_loop(0, nb, step, 0)

    for n in (6, 7):
        take(n)
    early = fill(EARLY, 2 * atoms)
    add_part(EARLY, 2 * atoms, early)
    for n in range(6):
        take(n)
    zcell[...] = nn(inner[...], hits(inner_len, z_row, 0)).astype(BF16)
    zcopy = pltpu.make_async_remote_copy(
        src_ref=zcell, dst_ref=zgot, send_sem=zsend, recv_sem=zrecv, device_id=partner, device_id_type=MESH)
    zcopy.start()
    late = fill(LATE, 2 * atoms + early)
    add_part(LATE, 2 * atoms + early, late)
    zhits[...] = hits(8 * rim_len, jnp.concatenate(columns_of, axis=1), 0)

    zcopy.wait_recv()
    cell = zgot[...]
    tail = cell[adim:].astype(F32)
    rows = lax.broadcasted_iota(I32, (3, zlen), 0)
    moved = tail[0:3] + tail[3:6] + jnp.where(rows == 2, (1 - 2 * k).astype(F32), 0.0)
    emb, place = columns(cell[0:adim], moved)
    wrt[:, 0:zlen] = emb
    tab[feat:, inner_len + shift_cols:] = place.astype(BF16)

    tens[...] = jnp.zeros_like(tens)

    def geometry(sep):
        sq = jnp.sum(sep * sep, axis=0, keepdims=True)
        inv = lax.rsqrt(sq + 0.25)
        dist = (sq + 0.25) * inv
        env = 1.0 / (1.0 + sq * sq * (1.0 / 16.0))
        radii = 0.5 + 0.4 * lax.broadcasted_iota(I32, (nbas, 1), 0).astype(F32)
        t = (dist - radii) * 2.0
        gauss = jnp.exp(-(t * t))
        return sq, inv, env, t, gauss

    def phase1(b, _):
        o_row = index_s[1:2, part(b)]
        a_c = one_c[:, part(b)]
        slab = hits(zlen, o_row, inner_len)
        tail = acc[feat:, part(b)] + nn(tab[feat:, inner_len + shift_cols:], slab)
        sep = tail[0:3] + tail[3:6] + tail[6:9]
        sq, inv, env, t, gauss = geometry(sep)
        radial = gauss * env
        r_hi = radial.astype(BF16).astype(F32)
        r_lo = radial - r_hi
        parts = jnp.concatenate([r_hi, r_lo, r_hi, r_lo], axis=0).astype(BF16)
        mixed = acc[0:feat, part(b)] + nn(wrt[...], jnp.concatenate([slab, parts], axis=0))
        s = sigmoid(mixed)
        latent = (mixed * s).astype(BF16)
        lat_s[:, part(b)] = latent
        dsilu_s[:, part(b)] = (s * (1.0 + mixed * (1.0 - s))).astype(BF16)
        chan = nn(w_chan_ref[...], latent)
        chan_s[:, part(b)] = chan
        dirs = sep * inv
        x, y, z = dirs[0:1], dirs[1:2], dirs[2:3]
        harm = jnp.concatenate([
            jnp.ones_like(x), x, y, z, ROOT3 * x * y, ROOT3 * y * z, ROOT3 * z * x,
            0.5 * ROOT3 * (x * x - y * y), 0.5 * (3.0 * z * z - 1.0),
            sep, env, jnp.zeros((3, block), F32)], axis=0)
        geo_s[:, part(b)] = harm
        prod = jnp.concatenate([chan] + [chan * harm[m:m + 1] for m in range(1, 9)], axis=0).astype(BF16)
        tens[0:9 * ch] += nt(prod, a_c)
        return 0

    lax.fori_loop(0, nb, phase1, 0)
    tens_b[...] = (0.125 * tens[0:9 * ch]).astype(BF16)
    tens[...] = jnp.zeros_like(tens)

    def phase2(b, _):
        a_c = one_c[:, part(b)]
        harm = geo_s[:, part(b)]
        env = harm[12:13]
        gath = nn(tens_b[...], a_c)
        g = [gath[m * ch:(m + 1) * ch] for m in range(9)]
        h = [harm[m:m + 1] for m in range(9)]
        inv0 = g[0]
        inv1 = g[1] * h[1] + g[2] * h[2] + g[3] * h[3]
        inv2 = g[4] * h[4] + g[5] * h[5] + g[6] * h[6] + g[7] * h[7] + g[8] * h[8]
        invb = jnp.concatenate([inv0, inv1, inv2], axis=0).astype(BF16)
        pre = nn(wcat[...], jnp.concatenate([lat_s[:, part(b)], invb], axis=0))
        s = sigmoid(pre)
        wo = wout_c[...]
        e = jnp.sum(pre * s * wo, axis=0, keepdims=True)
        dpre = (s * (1.0 + pre * (1.0 - s))) * wo * env
        back = nn(wback[...], dpre.astype(BF16))
        acc[0:feat, part(b)] = back[0:feat]
        dinv = [back[feat + l * ch:feat + (l + 1) * ch] for l in range(3)]
        dh = [jnp.sum(dinv[BANDS[m]] * g[m], axis=0, keepdims=True) for m in range(1, 9)]
        en = e * env
        dh_s[:, part(b)] = jnp.concatenate([e] + dh + [jnp.zeros((7, block), F32)], axis=0)
        en_hi = en.astype(BF16).astype(F32)
        prod = jnp.concatenate(
            [dinv[0]] + [dinv[BANDS[m]] * h[m] for m in range(1, 9)] + [en_hi, en - en_hi, jnp.zeros((14, block), F32)],
            axis=0).astype(BF16)
        tens[...] += nt(prod, a_c)
        return 0

    lax.fori_loop(0, nb, phase2, 0)
    out_ref[3] = tens[9 * ch:9 * ch + 1] + tens[9 * ch + 1:9 * ch + 2]
    tens_b[...] = (0.125 * tens[0:9 * ch]).astype(BF16)
    grad[...] = jnp.zeros_like(grad)
    q_order = list(range(nqc)) + [nqc + slot for slot in SLOT_ORDER] + [nqc + 16]
    nqo = len(q_order)

    def phase3(b, _):
        a_c = one_c[:, part(b)]
        harm = geo_s[:, part(b)]
        gd = nn(tens_b[...], a_c)
        g = [gd[m * ch:(m + 1) * ch] for m in range(9)]
        h = [harm[m:m + 1] for m in range(9)]
        chan = chan_s[:, part(b)]
        dchan = g[0]
        for m in range(1, 9):
            dchan = dchan + g[m] * h[m]
        old = dh_s[:, part(b)]
        d = [None] + [old[m:m + 1] + jnp.sum(chan * g[m], axis=0, keepdims=True) for m in range(1, 9)]
        dlat = acc[0:feat, part(b)] + nn(wchan[...], dchan.astype(BF16))
        dmixed = (dlat * dsilu_s[:, part(b)].astype(F32)).astype(BF16)
        d16 = nn(wr2[...], dmixed)
        drad = d16[0:nbas] + d16[nbas:]
        sep = harm[9:12]
        sq, inv, env, t, gauss = geometry(sep)
        dg = drad * gauss
        d_dist = jnp.sum(dg * t, axis=0, keepdims=True) * (-4.0 * env)
        d_env = jnp.sum(dg, axis=0, keepdims=True) + old[0:1]
        x, y, z = h[1], h[2], h[3]
        dx = d[1] + ROOT3 * (y * d[4] + z * d[6] + x * d[7])
        dy = d[2] + ROOT3 * (x * d[4] + z * d[5] - y * d[7])
        dz = d[3] + ROOT3 * (y * d[5] + x * d[6]) + 3.0 * z * d[8]
        d_dist = d_dist - (dx * x + dy * y + dz * z) * inv
        d_sq = d_dist * (0.5 * inv) - d_env * env * env * sq * 0.125
        dsep = jnp.concatenate([dx, dy, dz], axis=0) * inv + sep * (2.0 * d_sq)
        hi = dsep.astype(BF16).astype(F32)
        d8 = jnp.concatenate([hi, dsep - hi, jnp.zeros((2, block), F32)], axis=0)
        c_row, o_row = index_s[0:1, part(b)], index_s[1:2, part(b)]
        oq, cq = o_row >> 7, c_row >> 7
        lhs = jnp.concatenate(
            [jnp.where(oq == q, d8, 0.0) for q in q_order] + [jnp.where(cq == q, d8, 0.0) for q in range(nqc)],
            axis=0).astype(BF16)
        rhs = jnp.concatenate([hits(128, o_row & 127, 0), hits(128, c_row & 127, 0)], axis=0)
        grad[...] += nt(lhs, rhs)
        return 0

    lax.fori_loop(0, nb, phase3, 0)

    def summed(rows):
        return rows[0:3] + rows[3:6]

    first_of = {}
    rows = nqc
    for n, shift in enumerate(NEAR):
        first_of[n] = rows
        rows += len(CELLS[shift])
    def back_copy(n):
        sx, sy = NEAR[n]
        count = len(CELLS[sx, sy])
        return pltpu.make_async_remote_copy(
            src_ref=grad.at[first_of[n] * 8:(first_of[n] + count) * 8, 0:128], dst_ref=back_got.at[n, 0:count * 8],
            send_sem=bsend.at[n], recv_sem=brecv.at[n], device_id=at(sx, sy, k), device_id_type=MESH)

    def zback_copy(n):
        sx, sy = NEAR[n] if n < 8 else (0, 0)
        return pltpu.make_async_remote_copy(
            src_ref=grad.at[(nqo - 1) * 8:nqo * 8, 0:128], dst_ref=zback_got.at[n],
            send_sem=zbsend.at[n], recv_sem=zbrecv.at[n], device_id=at(sx, sy, 1 - k), device_id_type=MESH)

    for n in range(9):
        zback_copy(n).start()
        if n < 8:
            back_copy(n).start()

    def parts16(rows):
        return jnp.concatenate(list(three_parts(rows)) + [jnp.zeros((7, rows.shape[1]), F32)], axis=0).astype(BF16)

    def joined(rows):
        return rows[0:3] + rows[3:6] + rows[6:9]

    own_grad = jnp.concatenate(
        [summed(grad[q * 8:(q + 1) * 8, 0:128]) - summed(grad[(nqo + q) * 8:(nqo + q + 1) * 8, 128:256])
         for q in range(nqc)], axis=1)
    for n in range(9):
        zback_copy(n).wait_recv()
    slab_back = parts16(jnp.concatenate([summed(zback_got[n]) for n in range(8)], axis=1))
    rim_back = joined(nt(slab_back, zhits[...]))
    added = [jnp.zeros((3, rim_len), F32) for _ in range(8)]
    for n in range(8):
        back_copy(n).wait_recv()
        for m, (_, cell) in enumerate(CELLS[NEAR[n]]):
            added[cell] = added[cell] + summed(back_got[n, m * 8:(m + 1) * 8])
    rim_back = rim_back + jnp.concatenate(added, axis=1)
    last = jnp.concatenate([rim_back, summed(zback_got[8])], axis=1)
    own_grad = own_grad + joined(nt(parts16(last), rim_hits[...]))
    for c in range(3):
        out_ref[c] = -own_grad[c:c + 1]
    for n in range(8):
        rim_copy(n).wait_send()
        back_copy(n).wait_send()
    for n in range(9):
        zback_copy(n).wait_send()
    zcopy.wait_send()


def deal_kernel(result_ref, energy_ref, force_ref, sem):
    copies = [
        pltpu.make_async_copy(result_ref.at[3:4], energy_ref, sem.at[0]),
        pltpu.make_async_copy(result_ref.at[0:3], force_ref, sem.at[1])]
    for copy in copies:
        copy.start()
    for copy in copies:
        copy.wait()


def per_device(
    positions, attributes, edge_center, edge_other, edge_count, rim_rows, z_rows, w_emb, w_rbf, w_chan, w_lat, w_ten, w_out,
):
    atoms, adim = attributes.shape[3:]
    edges, (feat, ch) = edge_center.shape[3], w_chan.shape
    rim_len, zlen = rim_rows.shape[4], z_rows.shape[3]
    inner_len = atoms + 16 * rim_len
    tbl = inner_len + zlen
    V, D = pltpu.VMEM, pltpu.SemaphoreType.DMA
    arrays = (
        positions.reshape(3, 1, atoms), attributes.reshape(atoms, adim), rim_rows.reshape(8, rim_len),
        z_rows.reshape(1, zlen), edge_center.reshape(1, edges), edge_other.reshape(1, edges), edge_count.reshape(1, 1),
        w_emb, w_rbf, w_chan.T, w_lat, w_ten, w_out.reshape(1, feat))
    result = pl.pallas_call(
        functools.partial(whole_kernel, block=BLOCK),
        out_shape=jax.ShapeDtypeStruct((4, 1, atoms), F32),
        in_specs=[pl.BlockSpec(memory_space=pl.ANY)] * 13, out_specs=pl.BlockSpec(memory_space=pltpu.VMEM),
        scratch_shapes=[V(array.shape, array.dtype) for array in arrays] + [D((13,))] + [
            V((feat + 16, tbl + atoms), BF16), V((feat + 16, edges), F32), V((atoms, edges), BF16),
            V((feat, edges), BF16), V((feat, edges), BF16), V((ch, edges), F32), V((16, edges), F32), V((16, edges), F32),
            V((2, edges), I32), V((9 * ch + 16, atoms), F32), V((9 * ch, atoms), BF16),
            V(((tbl + atoms) // 128 * 8, 256), F32),
            V((feat, adim), BF16), V((feat, zlen + 32), BF16), V((feat, ch), BF16), V((feat, feat + 3 * ch), BF16),
            V((feat + 3 * ch, feat), BF16), V((16, feat), BF16), V((feat, 1), F32), V((atoms, 8 * rim_len + zlen), BF16),
            V((8 * rim_len, 8 * zlen), BF16),
            V((8, 3, adim + 16, rim_len), BF16), V((8, 3, adim + 16, rim_len), BF16), V((adim + 16, inner_len), BF16),
            V((adim + 16, zlen), BF16), V((adim + 16, zlen), BF16), V((9, 8, zlen), F32), V((8, 24, rim_len), F32),
            D((8,)), D((8,)), D, D, D((8,)), D((8,)), D((9,)), D((9,))],
        compiler_params=pltpu.CompilerParams(collective_id=0, has_side_effects=True, vmem_limit_bytes=VMEM_LIMIT),
        name="whole",
    )(*arrays)
    anywhere = pl.BlockSpec(memory_space=pl.ANY)
    energy, forces = pl.pallas_call(
        deal_kernel,
        out_shape=(jax.ShapeDtypeStruct((1, 1, atoms), F32), jax.ShapeDtypeStruct((3, 1, atoms), F32)),
        in_specs=[anywhere], out_specs=(anywhere, anywhere), scratch_shapes=[D((2,))], name="deal",
    )(result)
    return energy.reshape(1, 1, 1, atoms), forces.reshape(1, 1, 1, 3, atoms)


def solution(mesh):
    spread = P("gx", "gy", "gz")
    return jax.shard_map(
        per_device,
        mesh=mesh,
        in_specs=(spread,) * 7 + (P(),) * 6,
        out_specs=(spread, spread),
        check_vma=False,
    )
```

```python
import functools

import jax
import jax.numpy as jnp
from jax import lax
from jax.experimental import pallas as pl
from jax.experimental.pallas import tpu as pltpu
from jax.sharding import PartitionSpec as P

F32, BF16, I32 = jnp.float32, jnp.bfloat16, jnp.int32
ROOT3 = 3.0 ** 0.5
BANDS = (0, 1, 1, 1, 2, 2, 2, 2, 2)
BLOCK = 3072
VMEM_LIMIT = 62 << 20
MESH = pl.DeviceIdType.MESH
RIM_CELLS = [(0, 0), (0, 1), (0, 2), (1, 0), (1, 2), (2, 0), (2, 1), (2, 2)]


def source_of(position):
    if position == 0:
        return (-1, 2)
    if position == 4:
        return (1, 0)
    return (0, position - 1)


NEAR = [(0, 1), (0, -1), (1, 1), (1, -1), (-1, 1), (-1, -1), (1, 0), (-1, 0)]
CELLS = {shift: [] for shift in NEAR}
slots = 0
for row in range(5):
    for column in range(5):
        if row in (0, 4) or column in (0, 4):
            sx, ra = source_of(row)
            sy, rb = source_of(column)
            CELLS[sx, sy].append((slots, RIM_CELLS.index((ra, rb))))
            slots += 1
SLOT_ORDER = [slot for shift in NEAR for slot, _ in CELLS[shift]]
EARLY, MIDDLE, LATE = [(1, 3), (12, 3)], [(5, 6)], [(0, 1), (4, 1), (11, 1), (15, 1)]


def nt(a, b):
    return lax.dot_general(a, b, (((1,), (1,)), ((), ())), preferred_element_type=F32)


def nn(a, b):
    return jnp.dot(a, b, preferred_element_type=F32)


def turned(w, unit):
    return lax.dot_general(w, unit, (((0,), (0,)), ((), ())), preferred_element_type=F32).astype(BF16)


def sigmoid(x):
    return 0.5 * jnp.tanh(0.5 * x) + 0.5


def eye(n):
    rows = lax.broadcasted_iota(I32, (n, n), 0)
    cols = lax.broadcasted_iota(I32, (n, n), 1)
    return jnp.where(rows == cols, 1.0, 0.0).astype(BF16)


def three_parts(v):
    upper = v.astype(BF16).astype(F32)
    rest = v - upper
    middle = rest.astype(BF16).astype(F32)
    return upper, middle, rest - middle


def hits(rows, index_row, offset):
    width = index_row.shape[1]
    ids = lax.broadcasted_iota(jnp.int16, (rows, width), 0)
    wanted = jnp.broadcast_to((index_row - offset).astype(jnp.int16), (rows, width))
    return jnp.where(ids == wanted, jnp.ones((), BF16), jnp.zeros((), BF16))


def whole_kernel(*refs, block):
    sources, out_ref = refs[:13], refs[13]
    held, rest = refs[14:27], refs[27:]
    (pos_ref, attr_ref, rim_ref, z_ref, center_ref, other_ref, count_ref,
     w_emb_ref, w_rbf_ref, w_chan_ref, w_lat_ref, w_ten_ref, w_out_ref) = held
    (in_sem, tab, acc, one_c, lat_s, dsilu_s, chan_s, geo_s, dh_s, index_s, tens, tens_b, grad,
     emb_t, wrt, wchan, wcat, wback, wr2, wout_c, rim_hits, zhits,
     cells, got, inner, zcell, zgot, zback_got, back_got,
     send_sem, recv_sem, zsend, zrecv, bsend, brecv, zbsend, zbrecv) = rest

    def fetch(n):
        return pltpu.make_async_copy(sources[n], held[n], in_sem.at[n])

    adim, feat = w_emb_ref.shape
    ch, nbas = w_chan_ref.shape[0], w_rbf_ref.shape[0]
    atoms, edges = attr_ref.shape[0], center_ref.shape[1]
    rim_len, zlen = rim_ref.shape[1], z_ref.shape[1]
    inner_len = atoms + 16 * rim_len
    tbl = inner_len + zlen
    nb = edges // block
    nqc = atoms // 128

    i, j, k = (lax.axis_index(name) for name in ("gx", "gy", "gz"))
    nx, ny = lax.axis_size("gx"), lax.axis_size("gy")

    def at(sx, sy, side):
        return (lax.rem(i + (sx + nx), nx), lax.rem(j + (sy + ny), ny), side)

    partner = (i, j, 1 - k)
    barrier = pltpu.get_barrier_semaphore()
    for sx, sy in NEAR:
        pl.semaphore_signal(barrier, inc=1, device_id=at(sx, sy, k), device_id_type=MESH)
        pl.semaphore_signal(barrier, inc=1, device_id=at(sx, sy, 1 - k), device_id_type=MESH)
    pl.semaphore_signal(barrier, inc=1, device_id=partner, device_id_type=MESH)
    for n in range(13):
        fetch(n).start()
    for n in range(4):
        fetch(n).wait()

    pos = jnp.concatenate([pos_ref[0], pos_ref[1], pos_ref[2]], axis=0)
    upper = pos.astype(BF16).astype(F32)
    own = jnp.concatenate(
        [nt(eye(adim), attr_ref[...]), upper, pos - upper, jnp.zeros((10, atoms), F32)], axis=0).astype(BF16)
    inner[:, 0:atoms] = own
    rim_row = jnp.concatenate([rim_ref[c:c + 1, :] for c in range(8)], axis=1)
    rim_hits[:, 0:8 * rim_len] = hits(atoms, rim_row, 0)
    z_row = z_ref[...]
    z_rows = [(z_row >> 8).astype(F32), (z_row & 255).astype(F32)]
    packed = nn(own, rim_hits[:, 0:8 * rim_len])
    for n, shift in enumerate(NEAR):
        for m, (_, cell) in enumerate(CELLS[shift]):
            rows = packed[:, cell * rim_len:(cell + 1) * rim_len]
            cells[n, m] = jnp.concatenate([rows[0:adim + 6]] + z_rows + [rows[adim + 8:]], axis=0).astype(BF16)
    pl.semaphore_wait(barrier, 17)

    def rim_copy(n):
        sx, sy = NEAR[n]
        count = len(CELLS[sx, sy])
        return pltpu.make_async_remote_copy(
            src_ref=cells.at[n, 0:count], dst_ref=got.at[n, 0:count], send_sem=send_sem.at[n], recv_sem=recv_sem.at[n],
            device_id=at(-sx, -sy, k), device_id_type=MESH)

    for n in range(8):
        rim_copy(n).start()

    for n in range(4, 13):
        fetch(n).wait()
    big_eye = eye(feat)
    emb_t[...] = turned(w_emb_ref[...], eye(adim))
    wchan[...] = turned(w_chan_ref[...], eye(ch))
    wcat[:, 0:feat] = turned(w_lat_ref[...], big_eye)
    wcat[:, feat:] = turned(w_ten_ref[...], eye(3 * ch))
    wback[0:feat, :] = w_lat_ref[...]
    wback[feat:, :] = w_ten_ref[...]
    rb = w_rbf_ref[...]
    rb_hi = rb.astype(BF16).astype(F32)
    rb_lo = rb - rb_hi
    wr2[...] = jnp.concatenate([rb_hi, rb_lo], axis=0).astype(BF16)
    wrt[:, zlen:] = nt(big_eye, jnp.concatenate([rb_hi, rb_hi, rb_lo, rb_lo], axis=0).astype(BF16)).astype(BF16)
    diagonal = lax.broadcasted_iota(I32, (feat, feat), 0) == lax.broadcasted_iota(I32, (feat, feat), 1)
    wout_c[...] = jnp.sum(
        jnp.where(diagonal, jnp.broadcast_to(w_out_ref[...], (feat, feat)), 0.0), axis=1, keepdims=True)
    live = lax.broadcasted_iota(I32, (1, edges), 1) < count_ref[...]
    index_s[0:1, :] = jnp.where(live, center_ref[...], -1)
    index_s[1:2, :] = jnp.where(live, other_ref[...], -1)

    def columns(attr, place):
        emb = nn(emb_t[...], attr)
        emb = emb * sigmoid(emb)
        tail = jnp.zeros((7, place.shape[1]), F32)
        return emb.astype(BF16), jnp.concatenate(list(three_parts(place)) + [tail], axis=0)

    emb, place = columns(own[0:adim], pos)
    tab[0:feat, 0:atoms] = emb
    tab[0:feat, atoms:2 * atoms] = emb
    tab[feat:, 0:atoms] = place.astype(BF16)
    tab[feat:, atoms:2 * atoms] = (-place).astype(BF16)
    shift_cols = atoms

    def part(b):
        return pl.ds(pl.multiple_of(b * block, block), block)

    def own_part(b, _):
        c_row, o_row = index_s[0:1, part(b)], index_s[1:2, part(b)]
        a_c = hits(atoms, c_row, 0)
        one_c[:, part(b)] = a_c
        acc[:, part(b)] = nn(tab[:, 0:2 * atoms], jnp.concatenate([hits(atoms, o_row, 0), a_c], axis=0))
        return 0

    lax.fori_loop(0, nb, own_part, 0)

    rim_hits[:, 8 * rim_len:] = hits(atoms, z_row, 0)
    moved_at = {}
    columns_of = [None] * 8

    def take(n):
        rim_copy(n).wait_recv()
        sx, sy = NEAR[n]
        for m, (slot, _) in enumerate(CELLS[sx, sy]):
            cell = got[n, m]
            first = atoms + slot * rim_len
            tail = cell[adim:].astype(F32)
            rows = lax.broadcasted_iota(I32, (3, rim_len), 0)
            shift = jnp.where(rows == 0, float(sx), jnp.where(rows == 1, float(sy), 0.0))
            moved = tail[0:3] + tail[3:6] + shift
            moved_at[slot] = moved
            upper = moved.astype(BF16).astype(F32)
            inner[0:adim, first:first + rim_len] = cell[0:adim]
            inner[adim:, first:first + rim_len] = jnp.concatenate(
                [upper, moved - upper, jnp.zeros((10, rim_len), F32)], axis=0).astype(BF16)
        listed = (got[n, 0][adim + 6:adim + 7].astype(F32) * 256.0 + got[n, 0][adim + 7:adim + 8].astype(F32)).astype(I32)
        column = jnp.full_like(listed, -1)
        for slot, cell in CELLS[-sx, -sy]:
            row = listed - (atoms + slot * rim_len)
            column = jnp.where((row >= 0) & (row < rim_len), row + cell * rim_len, column)
        columns_of[NEAR.index((-sx, -sy))] = column

    def fill(runs, first):
        attr = jnp.concatenate(
            [inner[0:adim, atoms + r * rim_len:atoms + (r + c) * rim_len] for r, c in runs], axis=1)
        emb, place = columns(attr, jnp.concatenate([moved_at[r + q] for r, c in runs for q in range(c)], axis=1))
        width = emb.shape[1]
        tab[0:feat, first:first + width] = emb
        tab[feat:, first:first + width] = place.astype(BF16)
        return width

    def add_part(runs, first, width):
        def step(b, _):
            o_row = index_s[1:2, part(b)]
            picks = jnp.concatenate([hits(c * rim_len, o_row, atoms + r * rim_len) for r, c in runs], axis=0)
            acc[:, part(b)] += nn(tab[:, first:first + width], picks)
            return 0

        lax.fori_loop(0, nb, step, 0)

    for n in (6, 7):
        take(n)
    early = fill(EARLY, 2 * atoms)
    add_part(EARLY, 2 * atoms, early)
    for n in (0, 1):
        take(n)
    middle = fill(MIDDLE, 2 * atoms + early)
    add_part(MIDDLE, 2 * atoms + early, middle)
    for n in (2, 3, 4, 5):
        take(n)
    zcell[...] = nn(inner[...], hits(inner_len, z_row, 0)).astype(BF16)
    zcopy = pltpu.make_async_remote_copy(
        src_ref=zcell, dst_ref=zgot, send_sem=zsend, recv_sem=zrecv, device_id=partner, device_id_type=MESH)
    zcopy.start()
    late = fill(LATE, 2 * atoms + early + middle)
    add_part(LATE, 2 * atoms + early + middle, late)
    zhits[...] = hits(8 * rim_len, jnp.concatenate(columns_of, axis=1), 0)

    zcopy.wait_recv()
    cell = zgot[...]
    tail = cell[adim:].astype(F32)
    rows = lax.broadcasted_iota(I32, (3, zlen), 0)
    moved = tail[0:3] + tail[3:6] + jnp.where(rows == 2, (1 - 2 * k).astype(F32), 0.0)
    emb, place = columns(cell[0:adim], moved)
    wrt[:, 0:zlen] = emb
    tab[feat:, inner_len + shift_cols:] = place.astype(BF16)

    tens[...] = jnp.zeros_like(tens)

    def geometry(sep):
        sq = jnp.sum(sep * sep, axis=0, keepdims=True)
        inv = lax.rsqrt(sq + 0.25)
        dist = (sq + 0.25) * inv
        env = 1.0 / (1.0 + sq * sq * (1.0 / 16.0))
        radii = 0.5 + 0.4 * lax.broadcasted_iota(I32, (nbas, 1), 0).astype(F32)
        t = (dist - radii) * 2.0
        gauss = jnp.exp(-(t * t))
        return sq, inv, env, t, gauss

    def phase1(b, _):
        o_row = index_s[1:2, part(b)]
        a_c = one_c[:, part(b)]
        slab = hits(zlen, o_row, inner_len)
        tail = acc[feat:, part(b)] + nn(tab[feat:, inner_len + shift_cols:], slab)
        sep = tail[0:3] + tail[3:6] + tail[6:9]
        sq, inv, env, t, gauss = geometry(sep)
        radial = gauss * env
        r_hi = radial.astype(BF16).astype(F32)
        r_lo = radial - r_hi
        parts = jnp.concatenate([r_hi, r_lo, r_hi, r_lo], axis=0).astype(BF16)
        mixed = acc[0:feat, part(b)] + nn(wrt[...], jnp.concatenate([slab, parts], axis=0))
        s = sigmoid(mixed)
        latent = (mixed * s).astype(BF16)
        lat_s[:, part(b)] = latent
        dsilu_s[:, part(b)] = (s * (1.0 + mixed * (1.0 - s))).astype(BF16)
        chan = nn(w_chan_ref[...], latent)
        chan_s[:, part(b)] = chan
        dirs = sep * inv
        x, y, z = dirs[0:1], dirs[1:2], dirs[2:3]
        harm = jnp.concatenate([
            jnp.ones_like(x), x, y, z, ROOT3 * x * y, ROOT3 * y * z, ROOT3 * z * x,
            0.5 * ROOT3 * (x * x - y * y), 0.5 * (3.0 * z * z - 1.0),
            sep, env, jnp.zeros((3, block), F32)], axis=0)
        geo_s[:, part(b)] = harm
        prod = jnp.concatenate([chan] + [chan * harm[m:m + 1] for m in range(1, 9)], axis=0).astype(BF16)
        tens[0:9 * ch] += nt(prod, a_c)
        return 0

    lax.fori_loop(0, nb, phase1, 0)
    tens_b[...] = (0.125 * tens[0:9 * ch]).astype(BF16)
    tens[...] = jnp.zeros_like(tens)

    def phase2(b, _):
        a_c = one_c[:, part(b)]
        harm = geo_s[:, part(b)]
        env = harm[12:13]
        gath = nn(tens_b[...], a_c)
        g = [gath[m * ch:(m + 1) * ch] for m in range(9)]
        h = [harm[m:m + 1] for m in range(9)]
        inv0 = g[0]
        inv1 = g[1] * h[1] + g[2] * h[2] + g[3] * h[3]
        inv2 = g[4] * h[4] + g[5] * h[5] + g[6] * h[6] + g[7] * h[7] + g[8] * h[8]
        invb = jnp.concatenate([inv0, inv1, inv2], axis=0).astype(BF16)
        pre = nn(wcat[...], jnp.concatenate([lat_s[:, part(b)], invb], axis=0))
        s = sigmoid(pre)
        wo = wout_c[...]
        e = jnp.sum(pre * s * wo, axis=0, keepdims=True)
        dpre = (s * (1.0 + pre * (1.0 - s))) * wo * env
        back = nn(wback[...], dpre.astype(BF16))
        acc[0:feat, part(b)] = back[0:feat]
        dinv = [back[feat + l * ch:feat + (l + 1) * ch] for l in range(3)]
        dh = [jnp.sum(dinv[BANDS[m]] * g[m], axis=0, keepdims=True) for m in range(1, 9)]
        en = e * env
        dh_s[:, part(b)] = jnp.concatenate([e] + dh + [jnp.zeros((7, block), F32)], axis=0)
        en_hi = en.astype(BF16).astype(F32)
        prod = jnp.concatenate(
            [dinv[0]] + [dinv[BANDS[m]] * h[m] for m in range(1, 9)] + [en_hi, en - en_hi, jnp.zeros((14, block), F32)],
            axis=0).astype(BF16)
        tens[...] += nt(prod, a_c)
        return 0

    lax.fori_loop(0, nb, phase2, 0)
    out_ref[3] = tens[9 * ch:9 * ch + 1] + tens[9 * ch + 1:9 * ch + 2]
    tens_b[...] = (0.125 * tens[0:9 * ch]).astype(BF16)
    grad[...] = jnp.zeros_like(grad)
    q_order = list(range(nqc)) + [nqc + slot for slot in SLOT_ORDER] + [nqc + 16]
    nqo = len(q_order)

    def phase3(b, _):
        a_c = one_c[:, part(b)]
        harm = geo_s[:, part(b)]
        gd = nn(tens_b[...], a_c)
        g = [gd[m * ch:(m + 1) * ch] for m in range(9)]
        h = [harm[m:m + 1] for m in range(9)]
        chan = chan_s[:, part(b)]
        dchan = g[0]
        for m in range(1, 9):
            dchan = dchan + g[m] * h[m]
        old = dh_s[:, part(b)]
        d = [None] + [old[m:m + 1] + jnp.sum(chan * g[m], axis=0, keepdims=True) for m in range(1, 9)]
        dlat = acc[0:feat, part(b)] + nn(wchan[...], dchan.astype(BF16))
        dmixed = (dlat * dsilu_s[:, part(b)].astype(F32)).astype(BF16)
        d16 = nn(wr2[...], dmixed)
        drad = d16[0:nbas] + d16[nbas:]
        sep = harm[9:12]
        sq, inv, env, t, gauss = geometry(sep)
        dg = drad * gauss
        d_dist = jnp.sum(dg * t, axis=0, keepdims=True) * (-4.0 * env)
        d_env = jnp.sum(dg, axis=0, keepdims=True) + old[0:1]
        x, y, z = h[1], h[2], h[3]
        dx = d[1] + ROOT3 * (y * d[4] + z * d[6] + x * d[7])
        dy = d[2] + ROOT3 * (x * d[4] + z * d[5] - y * d[7])
        dz = d[3] + ROOT3 * (y * d[5] + x * d[6]) + 3.0 * z * d[8]
        d_dist = d_dist - (dx * x + dy * y + dz * z) * inv
        d_sq = d_dist * (0.5 * inv) - d_env * env * env * sq * 0.125
        dsep = jnp.concatenate([dx, dy, dz], axis=0) * inv + sep * (2.0 * d_sq)
        hi = dsep.astype(BF16).astype(F32)
        d8 = jnp.concatenate([hi, dsep - hi, jnp.zeros((2, block), F32)], axis=0)
        c_row, o_row = index_s[0:1, part(b)], index_s[1:2, part(b)]
        oq, cq = o_row >> 7, c_row >> 7
        lhs = jnp.concatenate(
            [jnp.where(oq == q, d8, 0.0) for q in q_order] + [jnp.where(cq == q, d8, 0.0) for q in range(nqc)],
            axis=0).astype(BF16)
        rhs = jnp.concatenate([hits(128, o_row & 127, 0), hits(128, c_row & 127, 0)], axis=0)
        grad[...] += nt(lhs, rhs)
        return 0

    lax.fori_loop(0, nb, phase3, 0)

    def summed(rows):
        return rows[0:3] + rows[3:6]

    first_of = {}
    rows = nqc
    for n, shift in enumerate(NEAR):
        first_of[n] = rows
        rows += len(CELLS[shift])
    def back_copy(n):
        sx, sy = NEAR[n]
        count = len(CELLS[sx, sy])
        return pltpu.make_async_remote_copy(
            src_ref=grad.at[first_of[n] * 8:(first_of[n] + count) * 8, 0:128], dst_ref=back_got.at[n, 0:count * 8],
            send_sem=bsend.at[n], recv_sem=brecv.at[n], device_id=at(sx, sy, k), device_id_type=MESH)

    def zback_copy(n):
        sx, sy = NEAR[n] if n < 8 else (0, 0)
        return pltpu.make_async_remote_copy(
            src_ref=grad.at[(nqo - 1) * 8:nqo * 8, 0:128], dst_ref=zback_got.at[n],
            send_sem=zbsend.at[n], recv_sem=zbrecv.at[n], device_id=at(sx, sy, 1 - k), device_id_type=MESH)

    for n in range(9):
        zback_copy(n).start()
        if n < 8:
            back_copy(n).start()

    def parts16(rows):
        return jnp.concatenate(list(three_parts(rows)) + [jnp.zeros((7, rows.shape[1]), F32)], axis=0).astype(BF16)

    def joined(rows):
        return rows[0:3] + rows[3:6] + rows[6:9]

    own_grad = jnp.concatenate(
        [summed(grad[q * 8:(q + 1) * 8, 0:128]) - summed(grad[(nqo + q) * 8:(nqo + q + 1) * 8, 128:256])
         for q in range(nqc)], axis=1)
    for n in range(9):
        zback_copy(n).wait_recv()
    slab_back = parts16(jnp.concatenate([summed(zback_got[n]) for n in range(8)], axis=1))
    rim_back = joined(nt(slab_back, zhits[...]))
    added = [jnp.zeros((3, rim_len), F32) for _ in range(8)]
    for n in range(8):
        back_copy(n).wait_recv()
        for m, (_, cell) in enumerate(CELLS[NEAR[n]]):
            added[cell] = added[cell] + summed(back_got[n, m * 8:(m + 1) * 8])
    rim_back = rim_back + jnp.concatenate(added, axis=1)
    last = jnp.concatenate([rim_back, summed(zback_got[8])], axis=1)
    own_grad = own_grad + joined(nt(parts16(last), rim_hits[...]))
    for c in range(3):
        out_ref[c] = -own_grad[c:c + 1]
    for n in range(8):
        rim_copy(n).wait_send()
        back_copy(n).wait_send()
    for n in range(9):
        zback_copy(n).wait_send()
    zcopy.wait_send()


def deal_kernel(result_ref, energy_ref, force_ref, sem):
    copies = [
        pltpu.make_async_copy(result_ref.at[3:4], energy_ref, sem.at[0]),
        pltpu.make_async_copy(result_ref.at[0:3], force_ref, sem.at[1])]
    for copy in copies:
        copy.start()
    for copy in copies:
        copy.wait()


def per_device(
    positions, attributes, edge_center, edge_other, edge_count, rim_rows, z_rows, w_emb, w_rbf, w_chan, w_lat, w_ten, w_out,
):
    atoms, adim = attributes.shape[3:]
    edges, (feat, ch) = edge_center.shape[3], w_chan.shape
    rim_len, zlen = rim_rows.shape[4], z_rows.shape[3]
    inner_len = atoms + 16 * rim_len
    tbl = inner_len + zlen
    V, D = pltpu.VMEM, pltpu.SemaphoreType.DMA
    arrays = (
        positions.reshape(3, 1, atoms), attributes.reshape(atoms, adim), rim_rows.reshape(8, rim_len),
        z_rows.reshape(1, zlen), edge_center.reshape(1, edges), edge_other.reshape(1, edges), edge_count.reshape(1, 1),
        w_emb, w_rbf, w_chan.T, w_lat, w_ten, w_out.reshape(1, feat))
    result = pl.pallas_call(
        functools.partial(whole_kernel, block=BLOCK),
        out_shape=jax.ShapeDtypeStruct((4, 1, atoms), F32),
        in_specs=[pl.BlockSpec(memory_space=pl.ANY)] * 13, out_specs=pl.BlockSpec(memory_space=pltpu.VMEM),
        scratch_shapes=[V(array.shape, array.dtype) for array in arrays] + [D((13,))] + [
            V((feat + 16, tbl + atoms), BF16), V((feat + 16, edges), F32), V((atoms, edges), BF16),
            V((feat, edges), BF16), V((feat, edges), BF16), V((ch, edges), F32), V((16, edges), F32), V((16, edges), F32),
            V((2, edges), I32), V((9 * ch + 16, atoms), F32), V((9 * ch, atoms), BF16),
            V(((tbl + atoms) // 128 * 8, 256), F32),
            V((feat, adim), BF16), V((feat, zlen + 32), BF16), V((feat, ch), BF16), V((feat, feat + 3 * ch), BF16),
            V((feat + 3 * ch, feat), BF16), V((16, feat), BF16), V((feat, 1), F32), V((atoms, 8 * rim_len + zlen), BF16),
            V((8 * rim_len, 8 * zlen), BF16),
            V((8, 3, adim + 16, rim_len), BF16), V((8, 3, adim + 16, rim_len), BF16), V((adim + 16, inner_len), BF16),
            V((adim + 16, zlen), BF16), V((adim + 16, zlen), BF16), V((9, 8, zlen), F32), V((8, 24, rim_len), F32),
            D((8,)), D((8,)), D, D, D((8,)), D((8,)), D((9,)), D((9,))],
        compiler_params=pltpu.CompilerParams(collective_id=0, has_side_effects=True, vmem_limit_bytes=VMEM_LIMIT),
        name="whole",
    )(*arrays)
    anywhere = pl.BlockSpec(memory_space=pl.ANY)
    energy, forces = pl.pallas_call(
        deal_kernel,
        out_shape=(jax.ShapeDtypeStruct((1, 1, atoms), F32), jax.ShapeDtypeStruct((3, 1, atoms), F32)),
        in_specs=[anywhere], out_specs=(anywhere, anywhere), scratch_shapes=[D((2,))], name="deal",
    )(result)
    return energy.reshape(1, 1, 1, atoms), forces.reshape(1, 1, 1, 3, atoms)


def solution(mesh):
    spread = P("gx", "gy", "gz")
    return jax.shard_map(
        per_device,
        mesh=mesh,
        in_specs=(spread,) * 7 + (P(),) * 6,
        out_specs=(spread, spread),
        check_vma=False,
    )
```
